512 devices in a mesh: depth: 4 (over x), rows: 128 (over y, z, core).
Axes of the slice: x: 4, y: 8, z: 8, core: 2. Of those that a mesh axis runs over, the one named last changes fastest.
Arguments:
- incident: bfloat16 [3, 2, 4096, 1024], P(None, None, 'rows'), may hold values from -6 to 6
- row_taps: bfloat16 [4, 3, 2, 33], P('depth'), may hold values from -0.75 to 0.75
- col_taps: bfloat16 [4, 3, 2, 127], P('depth'), may hold values from -0.375 to 0.375
- hogel_light: float32 [4, 3, 4096, 1024], P('depth', None, 'rows'), may hold values from -6 to 6
- silhouette: int32 [4, 4096, 64], P('depth', 'rows'), may hold values from 0 to 16
- fill_counts: int32 [4, 256], P('depth', 'rows'), may hold values from 1 to 64, 10240 in all within a row
- hogel_index: int32 [4, 256, 64], P('depth', 'rows'), may hold values from 0 to 63, each once within a row
Outputs:
- layer_fields: bfloat16 [4, 3, 2, 4096, 1024], P('depth', None, None, 'rows')
The draws below stay inside these ranges and needn't reach their ends.
Inputs may be any that keep to these rules, and one draw needn't show every extreme that they name: Each entry is the count of one hogel row, at most 64; for each layer l, the sum of fill_counts[l, g] over all 256 hogel rows g is 10240. `hogel_index`: each list names every position of its hogel row once.
All inputs are finite; a program needn't handle non-finite values. No bound on the sum of `fill_counts` on one device may be relied on, other than what follows from the above.
Results may differ from the reference program's by a relative error of at most 0.006.
Values may be sent and summed in bfloat16 or wider, within the bound.
A program may use at most 64 MiB of HBM per device.

```python
import math
import jax
import jax.numpy as jnp
import numpy as np
from jax import lax

HS = 16
KR = 16
KC = 63
COLORS = 3
ROWS_DEV = 32
COLS = 1024
LAYERS = 4
ROWS = 4096
HROWS = 256
NH = 64
FILLED = 10240
N_DEPTH = 4
N_ROWS = 128


def touch_ends(array, own_key, smallest, high):
    spot = [jax.random.randint(jax.random.fold_in(own_key, axis), (), 0, length) for axis, length in enumerate(array.shape)]
    longest = array.shape.index(max(array.shape))
    beside = spot[:longest] + [(spot[longest] + 1) % array.shape[longest]] + spot[longest + 1:]
    return array.at[tuple(spot)].set(smallest).at[tuple(beside)].set(high)


def block_scale(own_key, shape, cuts, least, top_value):
    factor_of, own = 1.0, jax.random.fold_in(own_key, 6)
    for axis_at, blocks in cuts:
        draws = jnp.exp(jax.random.uniform(jax.random.fold_in(own, axis_at), (blocks,), jnp.float32, least / len(cuts), top_value / len(cuts)))
        factor_of = factor_of * jnp.repeat(draws, shape[axis_at] // blocks).reshape([-1 if axis == axis_at else 1 for axis in range(len(shape))])
    return factor_of


def length_profile(number_of, total, bound, skew):
    portions = [(1 << 20) // math.isqrt(rank ** skew) + 1 for rank in range(2, number_of + 1)]
    surplus, holding = total - bound - (number_of - 1), [1] * (number_of - 1)
    while surplus > 0:
        movable = [i for i in range(number_of - 1) if holding[i] < bound]
        whole, left = sum([portions[i] for i in movable]), surplus
        for i in movable:
            extra = min(bound - holding[i], max(1, left * portions[i] // whole), surplus)
            holding[i] = holding[i] + extra
            surplus = surplus - extra
    return np.array([bound] + holding)


def ragged(stream_key, amount, total, most, slope):
    if amount == 2:
        one = jax.random.randint(stream_key, (), max(1, total - most), min(most, total - 1) + 1)
        return jnp.stack([one, total - one])
    sizes = jnp.asarray(length_profile(amount, total, most, slope), jnp.int32)
    twos = (amount - 1) // 2
    source_of, sink = sizes[1:1 + 2 * twos:2], sizes[2:2 + 2 * twos:2]
    room = jnp.minimum(source_of - 1, most - sink)
    passed = jax.random.randint(jax.random.fold_in(stream_key, 1), (twos,), 0, 1 << 20) % (room + 1)
    sizes = sizes.at[1:1 + 2 * twos:2].set(source_of - passed).at[2:2 + 2 * twos:2].set(sink + passed)
    return sizes[jax.random.permutation(jax.random.fold_in(stream_key, 2), amount)]


def gaussian(key, dims, width, most, split=(), held_as=jnp.bfloat16):
    gain = block_scale(key, dims, split, -0.22, 0.18) if split else 1.0
    result = jax.random.normal(key, dims, jnp.float32) * width * gain
    return jnp.minimum(jnp.maximum(result, -most), most).astype(held_as)


def setup_inputs(seed: int = 0) -> dict:
    key_of = jax.random.split(jax.random.key(seed), 8)
    return {
        "incident": gaussian(key_of[0], (COLORS, 2, ROWS, COLS), 1.0, 6.0, ((2, 128),)),
        "row_taps": gaussian(key_of[1], (LAYERS, COLORS, 2, 2 * KR + 1), (4 * KR + 2) ** -0.5, 0.75, ((0, 4),)),
        "col_taps": gaussian(key_of[2], (LAYERS, COLORS, 2, 2 * KC + 1), (4 * KC + 2) ** -0.5, 0.375, ((0, 4),)),
        "hogel_light": gaussian(key_of[3], (LAYERS, COLORS, ROWS, COLS), 1.0, 6.0, ((0, 4), (2, 128)), jnp.float32),
        "silhouette": touch_ends(jax.random.randint(key_of[4], (LAYERS, ROWS, NH), 0, HS + 1), jax.random.fold_in(key_of[4], 1), 0, HS).astype(jnp.int32),
        "fill_counts": jax.vmap(lambda own: ragged(own, HROWS, FILLED, NH, 2))(jax.random.split(key_of[5], LAYERS)).reshape((LAYERS, HROWS)).astype(jnp.int32),
        "hogel_index": jax.vmap(lambda own: jax.random.permutation(own, NH))(jax.random.split(key_of[6], LAYERS * HROWS)).reshape((LAYERS, HROWS, NH)).astype(jnp.int32),
    }


def dft_tables(size_now):
    counter = jnp.arange(size_now, dtype=jnp.int32)
    product = counter[:, None] * counter[None, :] % size_now
    angles = product.astype(jnp.float32) * (2.0 * math.pi / size_now)
    return (jnp.cos(angles) / math.sqrt(size_now), jnp.sin(angles) / math.sqrt(size_now))

def row_matrix(taps, height, reach):
    width_ext = height + 2 * reach
    offsets = jnp.arange(width_ext, dtype=jnp.int32)[None, :] - jnp.arange(height, dtype=jnp.int32)[:, None]
    inside = (offsets >= 0) & (offsets <= 2 * reach)
    picked = jnp.take(taps, jnp.clip(offsets, 0, 2 * reach), axis=1)
    banded = jnp.where(inside[None], picked, jnp.zeros_like(picked))
    upper = jnp.concatenate([banded[0], -banded[1]], axis=1)
    lower = jnp.concatenate([banded[1], banded[0]], axis=1)
    return jnp.concatenate([upper, lower], axis=0)

def column_matrix(taps, reach):
    source = (jnp.arange(3, dtype=jnp.int32)[:, None, None] - 1) * 128 + jnp.arange(128, dtype=jnp.int32)[None, :, None]
    offsets = source - jnp.arange(128, dtype=jnp.int32)[None, None, :]
    inside = jnp.abs(offsets) <= reach
    picked = jnp.take(taps, jnp.clip(offsets + reach, 0, 2 * reach), axis=1)
    blocks = jnp.where(inside[None], picked, jnp.zeros_like(picked))
    real_rows = blocks[0].reshape(384, 128)
    imag_rows = blocks[1].reshape(384, 128)
    upper = jnp.concatenate([real_rows, imag_rows], axis=1)
    lower = jnp.concatenate([-imag_rows, real_rows], axis=1)
    return jnp.concatenate([upper, lower], axis=0)

def apply_columns(rowed, col_mats):
    colour_count, _, height, col_count = rowed.shape
    tile_count = col_count // 128
    padded = jnp.pad(rowed, ((0, 0), (0, 0), (0, 0), (128, 128)))
    pieces = [padded[..., tile_shift * 128:tile_shift * 128 + col_count].reshape(colour_count, 2, height, tile_count, 128) for tile_shift in range(3)]
    stacked = jnp.stack(pieces, axis=2)
    windows = stacked.transpose(0, 3, 4, 1, 2, 5).reshape(colour_count, height * tile_count, 768)
    mixed_cols = jnp.einsum('kna,kab->knb', windows.astype(jnp.float32), col_mats.astype(jnp.float32))
    return mixed_cols.reshape(colour_count, height, tile_count, 2, 128).transpose(0, 3, 1, 2, 4).reshape(colour_count, 2, height, col_count)

def live_tiles(counts, index_list):
    positions = index_list.shape[1]
    slots = jnp.arange(positions, dtype=jnp.int32)
    named = (index_list[:, :, None] == slots[None, None, :]) & (slots[None, :, None] < counts[:, None, None])
    return jnp.any(named, axis=1)

def transparency(edges, hogel_size):
    expanded = jnp.repeat(edges, hogel_size, axis=1)
    within = jnp.arange(expanded.shape[1], dtype=jnp.int32) % hogel_size
    return (within[None, :] < expanded).astype(jnp.float32)

def stereo_field(light, live, hogel_size):
    colour_count, height, col_count = light.shape
    live_pix = jnp.repeat(jnp.repeat(live, hogel_size, axis=0), hogel_size, axis=1).astype(jnp.float32)
    masked = light * live_pix[None]
    cos_tab, sin_tab = dft_tables(hogel_size)
    left_mat = jnp.concatenate([cos_tab, -sin_tab], axis=0)
    groups = height // hogel_size
    blocked = masked.reshape(colour_count, groups, hogel_size, col_count)
    left_out = jnp.einsum('ah,kghc->kgac', left_mat, blocked, precision=lax.Precision.HIGHEST)
    tile_count = col_count // 128
    arranged = left_out.reshape(colour_count, groups, 2, hogel_size, tile_count, 128).transpose(0, 1, 3, 4, 2, 5).reshape(-1, 256)
    per_block = 128 // hogel_size
    cos_big = jnp.kron(jnp.eye(per_block, dtype=jnp.float32), cos_tab)
    sin_big = jnp.kron(jnp.eye(per_block, dtype=jnp.float32), sin_tab)
    right_mat = jnp.concatenate([jnp.concatenate([cos_big, -sin_big], axis=1), jnp.concatenate([sin_big, cos_big], axis=1)], axis=0)
    result_tiles = jnp.dot(arranged, right_mat, precision=lax.Precision.HIGHEST)
    return result_tiles.reshape(colour_count, groups, hogel_size, tile_count, 2, 128).transpose(0, 4, 1, 2, 3, 5).reshape(colour_count, 2, height, col_count)

def reference(incident, row_taps, col_taps, hogel_light, silhouette, fill_counts, hogel_index):
    field_in = incident
    outputs = []
    band_rows = ROWS_DEV + 2 * KR
    starts = (jnp.arange(N_ROWS, dtype=jnp.int32) * ROWS_DEV)[:, None] + jnp.arange(band_rows, dtype=jnp.int32)[None, :]
    for layer_now in range(N_DEPTH):
        row_mats = jnp.stack([row_matrix(row_taps[layer_now, colour], ROWS_DEV, KR) for colour in range(COLORS)])
        col_mats = jnp.stack([column_matrix(col_taps[layer_now, colour], KC) for colour in range(COLORS)])
        padded = jnp.pad(field_in, ((0, 0), (0, 0), (KR, KR), (0, 0)))
        windows = padded[:, :, starts, :]
        windows = windows.transpose(0, 2, 1, 3, 4).reshape(COLORS, N_ROWS, 2 * band_rows, COLS)
        rowed = jnp.einsum('kab,knbc->knac', row_mats.astype(jnp.float32), windows.astype(jnp.float32))
        rowed = rowed.astype(jnp.bfloat16).reshape(COLORS, N_ROWS, 2, ROWS_DEV, COLS).transpose(0, 2, 1, 3, 4).reshape(COLORS, 2, ROWS, COLS)
        columned = apply_columns(rowed, col_mats)
        clear = transparency(silhouette[layer_now], HS)
        live = live_tiles(fill_counts[layer_now], hogel_index[layer_now])
        stereo = stereo_field(hogel_light[layer_now], live, HS)
        field_in = (clear[None, None] * columned + stereo).astype(jnp.bfloat16)
        outputs.append(field_in)
    return jnp.stack(outputs)
```

```python
import math

import jax
import jax.numpy as jnp
import ml_dtypes
import numpy as np
from jax import lax
from jax.experimental import pallas as pl
from jax.experimental.pallas import tpu as pltpu
from jax.sharding import PartitionSpec as P

HS = 16
KR = 16
KC = 63
COLORS = 3
ROWS_DEV = 32
COLS = 1024
LAYERS = 4
NH = 64
TILES = COLS // 128
EXT = ROWS_DEV + 2 * KR
TABLE_SCALE = 1.132805
LIGHT_SCALE = 1.0 / (HS * TABLE_SCALE * TABLE_SCALE)
MESH = pl.DeviceIdType.MESH
F32 = jnp.float32
BF16 = jnp.bfloat16


def dft_constants():
    counter = np.arange(HS)
    angles = (counter[:, None] * counter[None, :] % HS) * (2.0 * math.pi / HS)
    cos_tab, sin_tab = TABLE_SCALE * np.cos(angles), TABLE_SCALE * np.sin(angles)
    groups, per_block = ROWS_DEV // HS, 128 // HS
    left = np.concatenate([np.kron(np.eye(groups), cos_tab), np.kron(np.eye(groups), -sin_tab)], axis=0)
    cos_big, sin_big = np.kron(np.eye(per_block), cos_tab), np.kron(np.eye(per_block), sin_tab)
    right = np.block([[cos_big, -sin_big], [sin_big, cos_big]])
    return left.astype(ml_dtypes.bfloat16), right.astype(ml_dtypes.bfloat16)


def dot(a, b):
    return jnp.dot(a, b, preferred_element_type=F32)


def iota(shape, dim):
    return lax.broadcasted_iota(jnp.int32, shape, dim)


def kernel(
    inc, row_taps, col_taps, light, sil, counts, index, left, right, out,
    field, lights, meta, light_in, rt_in, ct_in, sil_in, cnt_in, idx_in, left_in, right_in,
    taps, expand, row_mat, col_mat, clear, stereo, vpad, mixed,
    load_sem, halo_send, halo_recv, light_send, light_recv, meta_send, meta_recv, ready, out_sem,
):
    depth, rows = lax.axis_index("depth"), lax.axis_index("rows")
    last = lax.axis_size("rows") - 1
    planes = lax.axis_size("depth")

    barrier = pltpu.get_barrier_semaphore()

    @pl.when(rows > 0)
    def _():
        pl.semaphore_signal(barrier, inc=1, device_id=(depth, rows - 1), device_id_type=MESH)

    for back in range(1, LAYERS):
        @pl.when(depth >= back)
        def _():
            pl.semaphore_signal(barrier, inc=1, device_id=(depth - back, rows), device_id_type=MESH)

    loads = []
    pairs = [(inc.at[c], field.at[0, c, :, pl.ds(KR, ROWS_DEV), :]) for c in range(COLORS)]
    pairs += [(light.at[0, c], light_in.at[c]) for c in range(COLORS)]
    pairs += [(index, idx_in), (counts, cnt_in), (col_taps, ct_in), (row_taps, rt_in), (sil, sil_in)]
    pairs += [(left, left_in), (right, right_in)]
    for i, (src, dst) in enumerate(pairs):
        copy = pltpu.make_async_copy(src, dst, load_sem.at[i])
        copy.start()
        loads.append(copy)
    load_inc, load_light = loads[:COLORS], loads[COLORS : 2 * COLORS]
    load_idx, load_cnt, load_ct, load_rt, load_sil, load_left, load_right = loads[2 * COLORS :]

    @pl.when(rows == 0)
    def _():
        field[:, :, :, 0:KR, :] = jnp.zeros((LAYERS + 1, COLORS, 2, KR, COLS), BF16)

    @pl.when(rows == last)
    def _():
        field[:, :, :, KR + ROWS_DEV :, :] = jnp.zeros((LAYERS + 1, COLORS, 2, KR, COLS), BF16)

    greetings = planes - 1 - depth + jnp.where(rows < last, 1, 0)

    @pl.when(greetings > 0)
    def _():
        pl.semaphore_wait(barrier, greetings)

    @pl.when(rows < last)
    def _():
        pl.semaphore_signal(ready, inc=1, device_id=(depth, rows + 1), device_id_type=MESH)

    def halo_down(l, c):
        return pltpu.make_async_remote_copy(
            src_ref=field.at[l, c, :, pl.ds(KR, KR), :],
            dst_ref=field.at[l, c, :, pl.ds(KR + ROWS_DEV, KR), :],
            send_sem=halo_send.at[l, c, 0], recv_sem=halo_recv.at[l, c, 0],
            device_id=(depth, jnp.maximum(rows - 1, 0)), device_id_type=MESH,
        )

    def halo_up(l, c):
        return pltpu.make_async_remote_copy(
            src_ref=field.at[l, c, :, pl.ds(ROWS_DEV, KR), :],
            dst_ref=field.at[l, c, :, pl.ds(0, KR), :],
            send_sem=halo_send.at[l, c, 1], recv_sem=halo_recv.at[l, c, 1],
            device_id=(depth, jnp.minimum(rows + 1, last)), device_id_type=MESH,
        )

    for c in range(COLORS):
        load_inc[c].wait()

        @pl.when(rows < last)
        def _():
            halo_up(0, c).start()

    expand[...] = jnp.where(
        lax.shift_right_logical(iota((NH, COLS), 1), 4) == iota((NH, COLS), 0), 1.0, 0.0
    ).astype(BF16)
    load_idx.wait()
    load_cnt.wait()
    live = []
    for g in range(ROWS_DEV // HS):
        named = (idx_in[0, g : g + 1, :] == iota((NH, NH), 0)) & (iota((NH, NH), 1) < cnt_in[0:1, g : g + 1])
        spots = lax.dot_general(
            jnp.ones((HS, NH), BF16), jnp.where(named, 1.0, 0.0).astype(BF16),
            (((1,), (1,)), ((), ())), preferred_element_type=F32,
        )
        live.append(dot(spots.astype(BF16), expand[...]))
    live = jnp.concatenate(live, axis=0) * LIGHT_SCALE

    def light_copy(c, dest):
        return pltpu.make_async_remote_copy(
            src_ref=lights.at[depth, c], dst_ref=lights.at[depth, c],
            send_sem=light_send.at[dest, c], recv_sem=light_recv.at[depth, c],
            device_id=(jnp.minimum(dest, planes - 1), rows), device_id_type=MESH,
        )

    def meta_copy(dest):
        return pltpu.make_async_remote_copy(
            src_ref=meta.at[depth], dst_ref=meta.at[depth],
            send_sem=meta_send.at[dest], recv_sem=meta_recv.at[depth],
            device_id=(jnp.minimum(dest, planes - 1), rows), device_id_type=MESH,
        )

    load_ct.wait()
    load_rt.wait()
    load_sil.wait()
    taps[...] = jnp.zeros_like(taps)
    for c in range(COLORS):
        taps[2 * c : 2 * c + 2, 0 : 2 * KC + 1] = ct_in[0, c].astype(F32)
        taps[8 + 2 * c : 10 + 2 * c, 0 : 2 * KR + 1] = rt_in[0, c].astype(F32)
    flip = jnp.where(iota((128, 128), 0) + iota((128, 128), 1) == 2 * KC + 1, 1.0, 0.0).astype(BF16)
    turned = dot(taps[0:8, :].astype(BF16), flip)
    plain = taps[8:16, :]
    shifted = pltpu.roll(plain, 64, 1)
    for c in range(COLORS):
        re, im = slice(2 * c, 2 * c + 1), slice(2 * c + 1, 2 * c + 2)
        taps[8 + 2 * c : 9 + 2 * c, :] = plain[re] - shifted[im]
        taps[9 + 2 * c : 10 + 2 * c, :] = plain[im] + shifted[re]
    taps[0:8, :] = turned
    meta[depth] = jnp.zeros((ROWS_DEV + HS, 128), BF16)
    meta[depth, 0:ROWS_DEV, 0:NH] = sil_in[0].astype(F32).astype(BF16)
    meta[depth, ROWS_DEV:, :] = taps[...].astype(BF16)
    for dest in range(LAYERS - 1, 0, -1):
        @pl.when(depth < dest)
        def _():
            meta_copy(dest).start()
    for c in range(COLORS):
        load_light[c].wait()
        lights[depth, c] = (light_in[c] * live).astype(BF16)
        for dest in range(LAYERS - 1, 0, -1):
            @pl.when(depth < dest)
            def _():
                light_copy(c, dest).start()

    @pl.when(rows > 0)
    def _():
        pl.semaphore_wait(ready, 1)
        for c in range(COLORS):
            halo_down(0, c).start()

    def matrices(l):
        @pl.when(l < depth)
        def _():
            pltpu.make_async_remote_copy(
                src_ref=meta.at[l], dst_ref=meta.at[l], send_sem=meta_send.at[0], recv_sem=meta_recv.at[l],
                device_id=(depth, rows), device_id_type=MESH,
            ).wait_recv()
        edges = dot(meta[l, 0:ROWS_DEV, 0:NH], expand[...])
        within = (iota((ROWS_DEV, COLS), 1) & (HS - 1)).astype(F32)
        clear[...] = jnp.where(within < edges, 1.0, 0.0)
        lines = meta[l, ROWS_DEV:, :].astype(F32)
        below = iota((128, 128), 0) > iota((128, 128), 1)
        above = iota((128, 128), 0) < iota((128, 128), 1)
        for c in range(COLORS):
            for comp in range(2):
                line = lines[8 + 2 * c + comp : 9 + 2 * c + comp]
                row_mat[c, ROWS_DEV * comp : ROWS_DEV * (comp + 1), :] = pltpu.roll(
                    jnp.broadcast_to(line, (ROWS_DEV, 128)), 0, 1, stride=1, stride_axis=0
                ).astype(BF16)
            turn = [
                pltpu.roll(
                    jnp.broadcast_to(lines[2 * c + comp : 2 * c + comp + 1], (128, 128)),
                    0, 1, stride=1, stride_axis=0,
                )
                for comp in range(2)
            ]
            for half, inside in enumerate((below, above)):
                real = jnp.where(inside, turn[0], 0.0)
                imag = jnp.where(inside, turn[1], 0.0)
                top, low = 128 * half, 256 + 128 * half
                col_mat[c, top : top + 128, 0:128] = real.astype(BF16)
                col_mat[c, top : top + 128, 128:256] = imag.astype(BF16)
                col_mat[c, low : low + 128, 0:128] = (-imag).astype(BF16)
                col_mat[c, low : low + 128, 128:256] = real.astype(BF16)

    def make_stereo(l, c):
        @pl.when(l < depth)
        def _():
            pltpu.make_async_remote_copy(
                src_ref=lights.at[l, c], dst_ref=lights.at[l, c],
                send_sem=light_send.at[0, c], recv_sem=light_recv.at[l, c],
                device_id=(depth, rows), device_id_type=MESH,
            ).wait_recv()
        half_done = dot(left_in[...], lights[l, c]).astype(BF16)
        for t in range(TILES):
            here = slice(128 * t, 128 * (t + 1))
            mixed[c, ROWS_DEV * t : ROWS_DEV * (t + 1), 0:128] = half_done[0:ROWS_DEV, here]
            mixed[c, ROWS_DEV * t : ROWS_DEV * (t + 1), 128:256] = half_done[ROWS_DEV:, here]
        done = dot(mixed[c], right_in[...])
        for t in range(TILES):
            here = slice(128 * t, 128 * (t + 1))
            part = done[ROWS_DEV * t : ROWS_DEV * (t + 1)]
            stereo[c, 0, :, here] = part[:, 0:128]
            stereo[c, 1, :, here] = part[:, 128:256]

    def out_copy(c):
        return pltpu.make_async_copy(
            field.at[depth + 1, c, :, pl.ds(KR, ROWS_DEV), :], out.at[0, c], out_sem.at[c]
        )

    matrices(0)
    load_left.wait()
    load_right.wait()
    for c in range(COLORS):
        make_stereo(0, c)

    def layer(l, carry):
        for c in range(COLORS):
            @pl.when(rows > 0)
            def _():
                halo_up(l, c).wait_recv()

            @pl.when(rows < last)
            def _():
                halo_down(l, c).wait_recv()

            rowed = dot(row_mat[c], field[l, c].reshape(2 * EXT, COLS))
            wide = jnp.concatenate([rowed, jnp.zeros((2 * ROWS_DEV, 128), F32)], axis=1)
            vpad[c] = pltpu.roll(wide, 64, 1).astype(BF16)
            windows = jnp.concatenate(
                [
                    jnp.concatenate(
                        [vpad[c, 0:ROWS_DEV, 128 * t : 128 * t + 256], vpad[c, ROWS_DEV:, 128 * t : 128 * t + 256]],
                        axis=1,
                    )
                    for t in range(TILES)
                ],
                axis=0,
            )
            columned = dot(windows, col_mat[c])
            for t in range(TILES):
                here = slice(128 * t, 128 * (t + 1))
                part = columned[ROWS_DEV * t : ROWS_DEV * (t + 1)]
                for comp in range(2):
                    value = part[:, 128 * comp : 128 * (comp + 1)] * clear[:, here] + stereo[c, comp, :, here]
                    field[l + 1, c, comp, KR : KR + ROWS_DEV, here] = value.astype(BF16)

            @pl.when((l < depth) & (rows > 0))
            def _():
                halo_down(l + 1, c).start()

            @pl.when((l < depth) & (rows < last))
            def _():
                halo_up(l + 1, c).start()

            @pl.when(l == depth)
            def _():
                out_copy(c).start()

        @pl.when(l < depth)
        def _():
            matrices(l + 1)
            for c in range(COLORS):
                make_stereo(l + 1, c)

        return carry

    lax.fori_loop(0, depth + 1, layer, 0)

    for c in range(COLORS):
        out_copy(c).wait()

    def finish(l, carry):
        for c in range(COLORS):
            @pl.when(rows > 0)
            def _():
                halo_down(l, c).wait_send()

            @pl.when(rows < last)
            def _():
                halo_up(l, c).wait_send()

        return carry

    lax.fori_loop(0, depth + 1, finish, 0)
    for dest in range(1, LAYERS):
        @pl.when(depth < dest)
        def _():
            meta_copy(dest).wait_send()
            for c in range(COLORS):
                light_copy(c, dest).wait_send()


def body(incident, row_taps, col_taps, hogel_light, silhouette, fill_counts, hogel_index):
    left, right = dft_constants()
    anywhere = pl.BlockSpec(memory_space=pltpu.HBM)
    dma = pltpu.SemaphoreType.DMA
    return pl.pallas_call(
        kernel,
        name="hologram",
        out_shape=jax.ShapeDtypeStruct((1,) + incident.shape, BF16),
        in_specs=[anywhere] * 9,
        out_specs=anywhere,
        scratch_shapes=[
            pltpu.VMEM((LAYERS + 1, COLORS, 2, EXT, COLS), BF16),
            pltpu.VMEM((LAYERS, COLORS, ROWS_DEV, COLS), BF16),
            pltpu.VMEM((LAYERS, ROWS_DEV + HS, 128), BF16),
            pltpu.VMEM((COLORS, ROWS_DEV, COLS), F32),
            pltpu.VMEM(row_taps.shape, BF16),
            pltpu.VMEM(col_taps.shape, BF16),
            pltpu.VMEM(silhouette.shape, jnp.int32),
            pltpu.VMEM(fill_counts.shape, jnp.int32),
            pltpu.VMEM(hogel_index.shape, jnp.int32),
            pltpu.VMEM(left.shape, BF16),
            pltpu.VMEM(right.shape, BF16),
            pltpu.VMEM((16, 128), F32),
            pltpu.VMEM((NH, COLS), BF16),
            pltpu.VMEM((COLORS, 2 * ROWS_DEV, 128), BF16),
            pltpu.VMEM((COLORS, 512, 256), BF16),
            pltpu.VMEM((ROWS_DEV, COLS), F32),
            pltpu.VMEM((COLORS, 2, ROWS_DEV, COLS), F32),
            pltpu.VMEM((COLORS, 2 * ROWS_DEV, COLS + 128), BF16),
            pltpu.VMEM((COLORS, ROWS_DEV * TILES, 256), BF16),
            dma((13,)),
            dma((LAYERS, COLORS, 2)),
            dma((LAYERS, COLORS, 2)),
            dma((LAYERS, COLORS)),
            dma((LAYERS, COLORS)),
            dma((LAYERS,)),
            dma((LAYERS,)),
            pltpu.SemaphoreType.REGULAR,
            dma((COLORS,)),
        ],
        compiler_params=pltpu.CompilerParams(
            collective_id=0, has_side_effects=True, vmem_limit_bytes=60 << 20
        ),
    )(
        incident, row_taps, col_taps, hogel_light, silhouette, fill_counts, hogel_index,
        jnp.asarray(left), jnp.asarray(right),
    )


def solution(mesh):
    placed = (
        P(None, None, "rows", None),
        P("depth", None, None, None),
        P("depth", None, None, None),
        P("depth", None, "rows", None),
        P("depth", "rows", None),
        P("depth", "rows"),
        P("depth", "rows", None),
    )
    return jax.shard_map(
        body,
        mesh=mesh,
        in_specs=placed,
        out_specs=P("depth", None, None, "rows", None),
        check_vma=False,
    )
```

```python
import math

import jax
import jax.numpy as jnp
import ml_dtypes
import numpy as np
from jax import lax
from jax.experimental import pallas as pl
from jax.experimental.pallas import tpu as pltpu
from jax.sharding import PartitionSpec as P

HS = 16
KR = 16
KC = 63
COLORS = 3
ROWS_DEV = 32
COLS = 1024
LAYERS = 4
NH = 64
TILES = COLS // 128
EXT = ROWS_DEV + 2 * KR
TABLE_SCALE = 1.132805
LIGHT_SCALE = 1.0 / (HS * TABLE_SCALE * TABLE_SCALE)
MESH = pl.DeviceIdType.MESH
F32 = jnp.float32
BF16 = jnp.bfloat16


def dft_constants():
    counter = np.arange(HS)
    angles = (counter[:, None] * counter[None, :] % HS) * (2.0 * math.pi / HS)
    cos_tab, sin_tab = TABLE_SCALE * np.cos(angles), TABLE_SCALE * np.sin(angles)
    groups, per_block = ROWS_DEV // HS, 128 // HS
    left = np.concatenate([np.kron(np.eye(groups), cos_tab), np.kron(np.eye(groups), -sin_tab)], axis=0)
    cos_big, sin_big = np.kron(np.eye(per_block), cos_tab), np.kron(np.eye(per_block), sin_tab)
    right = np.block([[cos_big, -sin_big], [sin_big, cos_big]])
    return left.astype(ml_dtypes.bfloat16), right.astype(ml_dtypes.bfloat16)


def dot(a, b):
    return jnp.dot(a, b, preferred_element_type=F32)


def iota(shape, dim):
    return lax.broadcasted_iota(jnp.int32, shape, dim)


def kernel(
    inc, row_taps, col_taps, light, sil, counts, index, left, right, out,
    field, lights, meta, light_in, rt_in, ct_in, sil_in, cnt_in, idx_in, left_in, right_in,
    taps, expand, row_mat, col_mat, clear, vpad, mixed,
    load_sem, halo_send, halo_recv, light_send, light_recv, meta_send, meta_recv, ready, relay,
):
    depth, rows = lax.axis_index("depth"), lax.axis_index("rows")
    last = lax.axis_size("rows") - 1
    planes = lax.axis_size("depth")

    barrier = pltpu.get_barrier_semaphore()

    @pl.when(rows > 0)
    def _():
        pl.semaphore_signal(barrier, inc=1, device_id=(depth, rows - 1), device_id_type=MESH)

    for back in range(1, LAYERS):
        @pl.when(depth >= back)
        def _():
            pl.semaphore_signal(barrier, inc=1, device_id=(depth - back, rows), device_id_type=MESH)

    loads = []
    pairs = [(inc.at[c], field.at[0, c, :, pl.ds(KR, ROWS_DEV), :]) for c in range(COLORS)]
    pairs += [(light.at[0, c], light_in.at[c]) for c in range(COLORS)]
    pairs += [(index, idx_in), (counts, cnt_in), (col_taps, ct_in), (row_taps, rt_in), (sil, sil_in)]
    pairs += [(left, left_in), (right, right_in)]
    for i, (src, dst) in enumerate(pairs):
        copy = pltpu.make_async_copy(src, dst, load_sem.at[i])
        copy.start()
        loads.append(copy)
    load_inc, load_light = loads[:COLORS], loads[COLORS : 2 * COLORS]
    load_idx, load_cnt, load_ct, load_rt, load_sil, load_left, load_right = loads[2 * COLORS :]

    @pl.when(rows == 0)
    def _():
        field[:, :, :, 0:KR, :] = jnp.zeros((LAYERS + 1, COLORS, 2, KR, COLS), BF16)

    @pl.when(rows == last)
    def _():
        field[:, :, :, KR + ROWS_DEV :, :] = jnp.zeros((LAYERS + 1, COLORS, 2, KR, COLS), BF16)

    greetings = planes - 1 - depth + jnp.where(rows < last, 1, 0)

    @pl.when(greetings > 0)
    def _():
        pl.semaphore_wait(barrier, greetings)

    @pl.when(rows < last)
    def _():
        pl.semaphore_signal(ready, inc=1, device_id=(depth, rows + 1), device_id_type=MESH)

    def halo_down(l, c):
        return pltpu.make_async_remote_copy(
            src_ref=field.at[l, c, :, pl.ds(KR, KR), :],
            dst_ref=field.at[l, c, :, pl.ds(KR + ROWS_DEV, KR), :],
            send_sem=halo_send.at[l, c, 0], recv_sem=halo_recv.at[l, c, 0],
            device_id=(depth, jnp.maximum(rows - 1, 0)), device_id_type=MESH,
        )

    def halo_up(l, c):
        return pltpu.make_async_remote_copy(
            src_ref=field.at[l, c, :, pl.ds(ROWS_DEV, KR), :],
            dst_ref=field.at[l, c, :, pl.ds(0, KR), :],
            send_sem=halo_send.at[l, c, 1], recv_sem=halo_recv.at[l, c, 1],
            device_id=(depth, jnp.minimum(rows + 1, last)), device_id_type=MESH,
        )

    for c in range(COLORS):
        load_inc[c].wait()

        @pl.when(rows < last)
        def _():
            halo_up(0, c).start()

    expand[...] = jnp.where(
        lax.shift_right_logical(iota((NH, COLS), 1), 4) == iota((NH, COLS), 0), 1.0, 0.0
    ).astype(BF16)
    load_idx.wait()
    load_cnt.wait()
    live = []
    for g in range(ROWS_DEV // HS):
        named = (idx_in[0, g : g + 1, :] == iota((NH, NH), 0)) & (iota((NH, NH), 1) < cnt_in[0:1, g : g + 1])
        spots = lax.dot_general(
            jnp.ones((HS, NH), BF16), jnp.where(named, 1.0, 0.0).astype(BF16),
            (((1,), (1,)), ((), ())), preferred_element_type=F32,
        )
        live.append(dot(spots.astype(BF16), expand[...]))
    live = jnp.concatenate(live, axis=0) * LIGHT_SCALE

    def light_copy(l, c, dest):
        return pltpu.make_async_remote_copy(
            src_ref=lights.at[l, c], dst_ref=lights.at[l, c],
            send_sem=light_send.at[LAYERS * l + dest, c], recv_sem=light_recv.at[l, c],
            device_id=(dest, rows), device_id_type=MESH,
        )

    def meta_copy(dest):
        return pltpu.make_async_remote_copy(
            src_ref=meta.at[depth], dst_ref=meta.at[depth],
            send_sem=meta_send.at[dest], recv_sem=meta_recv.at[depth],
            device_id=(jnp.minimum(dest, planes - 1), rows), device_id_type=MESH,
        )

    load_ct.wait()
    load_rt.wait()
    load_sil.wait()
    taps[...] = jnp.zeros_like(taps)
    for c in range(COLORS):
        taps[2 * c : 2 * c + 2, 0 : 2 * KC + 1] = ct_in[0, c].astype(F32)
        taps[8 + 2 * c : 10 + 2 * c, 0 : 2 * KR + 1] = rt_in[0, c].astype(F32)
    flip = jnp.where(iota((128, 128), 0) + iota((128, 128), 1) == 2 * KC + 1, 1.0, 0.0).astype(BF16)
    turned = dot(taps[0:8, :].astype(BF16), flip)
    plain = taps[8:16, :]
    shifted = pltpu.roll(plain, 64, 1)
    for c in range(COLORS):
        re, im = slice(2 * c, 2 * c + 1), slice(2 * c + 1, 2 * c + 2)
        taps[8 + 2 * c : 9 + 2 * c, :] = plain[re] - shifted[im]
        taps[9 + 2 * c : 10 + 2 * c, :] = plain[im] + shifted[re]
    taps[0:8, :] = turned
    meta[depth] = jnp.zeros((ROWS_DEV + HS, 128), BF16)
    meta[depth, 0:ROWS_DEV, 0:NH] = sil_in[0].astype(F32).astype(BF16)
    meta[depth, ROWS_DEV:, :] = taps[...].astype(BF16)
    for dest in range(LAYERS - 1, 0, -1):
        @pl.when(depth < dest)
        def _():
            meta_copy(dest).start()

    for c in range(COLORS):
        load_light[c].wait()
    for c in range(COLORS):
        lights[depth, c] = (light_in[c] * live).astype(BF16)

    @pl.when(depth == 0)
    def _():
        for c in range(COLORS):
            light_copy(0, c, 3).start()
            light_copy(0, c, 1).start()

    @pl.when(depth == 1)
    def _():
        for c in range(COLORS):
            light_copy(1, c, 2).start()

    @pl.when(depth == 2)
    def _():
        pl.semaphore_signal(relay, inc=1, device_id=(3, rows), device_id_type=MESH)
        for c in range(COLORS):
            light_copy(2, c, 3).start()

    @pl.when(rows > 0)
    def _():
        pl.semaphore_wait(ready, 1)
        for c in range(COLORS):
            halo_down(0, c).start()

    def matrices(l):
        @pl.when(l < depth)
        def _():
            pltpu.make_async_remote_copy(
                src_ref=meta.at[l], dst_ref=meta.at[l], send_sem=meta_send.at[0], recv_sem=meta_recv.at[l],
                device_id=(depth, rows), device_id_type=MESH,
            ).wait_recv()
        edges = dot(meta[l, 0:ROWS_DEV, 0:NH], expand[...])
        within = (iota((ROWS_DEV, COLS), 1) & (HS - 1)).astype(F32)
        clear[...] = jnp.where(within < edges, 1.0, 0.0)
        lines = meta[l, ROWS_DEV:, :].astype(F32)
        below = iota((128, 128), 0) > iota((128, 128), 1)
        above = iota((128, 128), 0) < iota((128, 128), 1)
        for c in range(COLORS):
            for comp in range(2):
                line = lines[8 + 2 * c + comp : 9 + 2 * c + comp]
                row_mat[c, ROWS_DEV * comp : ROWS_DEV * (comp + 1), :] = pltpu.roll(
                    jnp.broadcast_to(line, (ROWS_DEV, 128)), 0, 1, stride=1, stride_axis=0
                ).astype(BF16)
            turn = [
                pltpu.roll(
                    jnp.broadcast_to(lines[2 * c + comp : 2 * c + comp + 1], (128, 128)),
                    0, 1, stride=1, stride_axis=0,
                )
                for comp in range(2)
            ]
            for half, inside in enumerate((below, above)):
                real = jnp.where(inside, turn[0], 0.0)
                imag = jnp.where(inside, turn[1], 0.0)
                top, low = 128 * half, 256 + 128 * half
                col_mat[c, top : top + 128, 0:128] = real.astype(BF16)
                col_mat[c, top : top + 128, 128:256] = imag.astype(BF16)
                col_mat[c, low : low + 128, 0:128] = (-imag).astype(BF16)
                col_mat[c, low : low + 128, 128:256] = real.astype(BF16)

    def colour(l, c):
        @pl.when((l < depth) & ((depth != 2) | (l != 1)))
        def _():
            pltpu.make_async_remote_copy(
                src_ref=lights.at[l, c], dst_ref=lights.at[l, c],
                send_sem=light_send.at[0, c], recv_sem=light_recv.at[l, c],
                device_id=(depth, rows), device_id_type=MESH,
            ).wait_recv()

        @pl.when((l == 0) & (depth == 3))
        def _():
            light_copy(0, c, 2).start()
        @pl.when(rows > 0)
        def _():
            halo_up(l, c).wait_recv()

        @pl.when(rows < last)
        def _():
            halo_down(l, c).wait_recv()

        half_done = dot(left_in[...], lights[l, c]).astype(BF16)
        for t in range(TILES):
            here = slice(128 * t, 128 * (t + 1))
            mixed[c, ROWS_DEV * t : ROWS_DEV * (t + 1), 0:128] = half_done[0:ROWS_DEV, here]
            mixed[c, ROWS_DEV * t : ROWS_DEV * (t + 1), 128:256] = half_done[ROWS_DEV:, here]
        done = dot(mixed[c], right_in[...])
        rowed = dot(row_mat[c], field[l, c].reshape(2 * EXT, COLS))
        wide = jnp.concatenate([rowed, jnp.zeros((2 * ROWS_DEV, 128), F32)], axis=1)
        vpad[c] = pltpu.roll(wide, 64, 1).astype(BF16)
        windows = jnp.concatenate(
            [
                jnp.concatenate(
                    [vpad[c, 0:ROWS_DEV, 128 * t : 128 * t + 256], vpad[c, ROWS_DEV:, 128 * t : 128 * t + 256]],
                    axis=1,
                )
                for t in range(TILES)
            ],
            axis=0,
        )
        columned = dot(windows, col_mat[c])
        for t in range(TILES):
            here = slice(128 * t, 128 * (t + 1))
            band = slice(ROWS_DEV * t, ROWS_DEV * (t + 1))
            for comp in range(2):
                side = slice(128 * comp, 128 * (comp + 1))
                value = (columned[band, side] * clear[:, here] + done[band, side]).astype(BF16)
                field[l + 1, c, comp, KR : KR + ROWS_DEV, here] = value
                out[0, c, comp, :, here] = value

        @pl.when((l < depth) & (rows > 0))
        def _():
            halo_down(l + 1, c).start()

        @pl.when((l < depth) & (rows < last))
        def _():
            halo_up(l + 1, c).start()

    matrices(0)

    @pl.when(depth == 2)
    def _():
        for c in range(COLORS):
            light_copy(1, c, 2).wait_recv()
            light_copy(1, c, 3).start()

    @pl.when(depth == 3)
    def _():
        pl.semaphore_wait(relay, 1)

    load_left.wait()
    load_right.wait()
    for c in range(COLORS):
        colour(0, c)

    def layer(l, carry):
        matrices(l)
        for c in range(COLORS):
            colour(l, c)
        return carry

    lax.fori_loop(1, depth + 1, layer, 0)

    def finish(l, carry):
        for c in range(COLORS):
            @pl.when(rows > 0)
            def _():
                halo_down(l, c).wait_send()

            @pl.when(rows < last)
            def _():
                halo_up(l, c).wait_send()

        return carry

    lax.fori_loop(0, depth + 1, finish, 0)
    for dest in range(1, LAYERS):
        @pl.when(depth < dest)
        def _():
            meta_copy(dest).wait_send()

    for at, l, dest in ((0, 0, 3), (0, 0, 1), (1, 1, 2), (2, 2, 3), (2, 1, 3), (3, 0, 2)):
        @pl.when(depth == at)
        def _():
            for c in range(COLORS):
                light_copy(l, c, dest).wait_send()


def body(incident, row_taps, col_taps, hogel_light, silhouette, fill_counts, hogel_index):
    left, right = dft_constants()
    anywhere = pl.BlockSpec(memory_space=pltpu.HBM)
    dma = pltpu.SemaphoreType.DMA
    return pl.pallas_call(
        kernel,
        name="hologram",
        out_shape=jax.ShapeDtypeStruct((1,) + incident.shape, BF16),
        in_specs=[anywhere] * 9,
        out_specs=pl.BlockSpec(memory_space=pltpu.VMEM),
        scratch_shapes=[
            pltpu.VMEM((LAYERS + 1, COLORS, 2, EXT, COLS), BF16),
            pltpu.VMEM((LAYERS, COLORS, ROWS_DEV, COLS), BF16),
            pltpu.VMEM((LAYERS, ROWS_DEV + HS, 128), BF16),
            pltpu.VMEM((COLORS, ROWS_DEV, COLS), F32),
            pltpu.VMEM(row_taps.shape, BF16),
            pltpu.VMEM(col_taps.shape, BF16),
            pltpu.VMEM(silhouette.shape, jnp.int32),
            pltpu.VMEM(fill_counts.shape, jnp.int32),
            pltpu.VMEM(hogel_index.shape, jnp.int32),
            pltpu.VMEM(left.shape, BF16),
            pltpu.VMEM(right.shape, BF16),
            pltpu.VMEM((16, 128), F32),
            pltpu.VMEM((NH, COLS), BF16),
            pltpu.VMEM((COLORS, 2 * ROWS_DEV, 128), BF16),
            pltpu.VMEM((COLORS, 512, 256), BF16),
            pltpu.VMEM((ROWS_DEV, COLS), F32),
            pltpu.VMEM((COLORS, 2 * ROWS_DEV, COLS + 128), BF16),
            pltpu.VMEM((COLORS, ROWS_DEV * TILES, 256), BF16),
            dma((13,)),
            dma((LAYERS, COLORS, 2)),
            dma((LAYERS, COLORS, 2)),
            dma((LAYERS * LAYERS, COLORS)),
            dma((LAYERS, COLORS)),
            dma((LAYERS,)),
            dma((LAYERS,)),
            pltpu.SemaphoreType.REGULAR,
            pltpu.SemaphoreType.REGULAR,
        ],
        compiler_params=pltpu.CompilerParams(
            collective_id=0, has_side_effects=True, vmem_limit_bytes=40 << 20
        ),
    )(*[
        pltpu.with_memory_space_constraint(x, pltpu.HBM)
        for x in (
            incident, row_taps, col_taps, hogel_light, silhouette, fill_counts, hogel_index,
            jnp.asarray(left), jnp.asarray(right),
        )
    ])


def solution(mesh):
    placed = (
        P(None, None, "rows", None),
        P("depth", None, None, None),
        P("depth", None, None, None),
        P("depth", None, "rows", None),
        P("depth", "rows", None),
        P("depth", "rows"),
        P("depth", "rows", None),
    )
    return jax.shard_map(
        body,
        mesh=mesh,
        in_specs=placed,
        out_specs=P("depth", None, None, "rows", None),
        check_vma=False,
    )
```

```python
import math

import jax
import jax.numpy as jnp
import ml_dtypes
import numpy as np
from jax import lax
from jax.experimental import pallas as pl
from jax.experimental.pallas import tpu as pltpu
from jax.sharding import PartitionSpec as P

HS = 16
KR = 16
KC = 63
COLORS = 3
ROWS_DEV = 32
COLS = 1024
LAYERS = 4
NH = 64
TILES = COLS // 128
EXT = ROWS_DEV + 2 * KR
TABLE_SCALE = 1.132805
LIGHT_SCALE = 1.0 / (HS * TABLE_SCALE * TABLE_SCALE)
MESH = pl.DeviceIdType.MESH
F32 = jnp.float32
BF16 = jnp.bfloat16


def dft_constants():
    counter = np.arange(HS)
    angles = (counter[:, None] * counter[None, :] % HS) * (2.0 * math.pi / HS)
    cos_tab, sin_tab = TABLE_SCALE * np.cos(angles), TABLE_SCALE * np.sin(angles)
    groups, per_block = ROWS_DEV // HS, 128 // HS
    left = np.concatenate([np.kron(np.eye(groups), cos_tab), np.kron(np.eye(groups), -sin_tab)], axis=0)
    cos_big, sin_big = np.kron(np.eye(per_block), cos_tab), np.kron(np.eye(per_block), sin_tab)
    right = np.block([[cos_big, -sin_big], [sin_big, cos_big]])
    return left.astype(ml_dtypes.bfloat16), right.astype(ml_dtypes.bfloat16)


def dot(a, b):
    return jnp.dot(a, b, preferred_element_type=F32)


def iota(shape, dim):
    return lax.broadcasted_iota(jnp.int32, shape, dim)


def kernel(
    inc, row_taps, col_taps, light, sil, counts, index, left, right, out,
    field, broad, inner, lights, edge_light, meta, edge_meta,
    light_in, rt_in, ct_in, sil_in, cnt_in, idx_in, left_in, right_in,
    taps, expand, row_mat, row_wide, col_mat, clear, clear_wide, stereo, stereo_wide, vpad, vpad_wide, mixed,
    load_sem, halo_send, halo_recv, broad_send, broad_recv, edge_send, edge_recv,
    light_send, light_recv, meta_send, meta_recv, ready,
):
    depth, rows = lax.axis_index("depth"), lax.axis_index("rows")
    last = lax.axis_size("rows") - 1
    planes = lax.axis_size("depth")

    barrier = pltpu.get_barrier_semaphore()

    @pl.when(rows > 0)
    def _():
        pl.semaphore_signal(barrier, inc=1, device_id=(depth, rows - 1), device_id_type=MESH)

    for back in range(1, LAYERS):
        @pl.when(depth >= back)
        def _():
            pl.semaphore_signal(barrier, inc=1, device_id=(depth - back, rows), device_id_type=MESH)

    loads = []
    pairs = [(inc.at[c], field.at[0, c, :, pl.ds(KR, ROWS_DEV), :]) for c in range(COLORS)]
    pairs += [(light.at[0, c], light_in.at[c]) for c in range(COLORS)]
    pairs += [(index, idx_in), (counts, cnt_in), (col_taps, ct_in), (row_taps, rt_in), (sil, sil_in)]
    pairs += [(left, left_in), (right, right_in)]
    for i, (src, dst) in enumerate(pairs):
        copy = pltpu.make_async_copy(src, dst, load_sem.at[i])
        copy.start()
        loads.append(copy)
    load_inc, load_light = loads[:COLORS], loads[COLORS : 2 * COLORS]
    load_idx, load_cnt, load_ct, load_rt, load_sil, load_left, load_right = loads[2 * COLORS :]

    @pl.when(rows == 0)
    def _():
        field[:, :, :, 0:KR, :] = jnp.zeros((2, COLORS, 2, KR, COLS), BF16)
        broad[:, :, 0 : 2 * KR, :] = jnp.zeros((COLORS, 2, 2 * KR, COLS), BF16)
        edge_light[0] = jnp.zeros((COLORS, HS, COLS), BF16)
        edge_meta[0] = jnp.zeros((HS, 128), BF16)

    @pl.when(rows == last)
    def _():
        field[:, :, :, KR + ROWS_DEV :, :] = jnp.zeros((2, COLORS, 2, KR, COLS), BF16)
        broad[:, :, 2 * KR + ROWS_DEV :, :] = jnp.zeros((COLORS, 2, 2 * KR, COLS), BF16)
        edge_light[1] = jnp.zeros((COLORS, HS, COLS), BF16)
        edge_meta[1] = jnp.zeros((HS, 128), BF16)

    greetings = planes - 1 - depth + jnp.where(rows < last, 1, 0)

    @pl.when(greetings > 0)
    def _():
        pl.semaphore_wait(barrier, greetings)

    @pl.when(rows < last)
    def _():
        pl.semaphore_signal(ready, inc=1, device_id=(depth, rows + 1), device_id_type=MESH)

    def halo_down(l, c):
        return pltpu.make_async_remote_copy(
            src_ref=field.at[l, c, :, pl.ds(KR, KR), :] if l else inc.at[c, :, pl.ds(0, KR), :],
            dst_ref=field.at[l, c, :, pl.ds(KR + ROWS_DEV, KR), :],
            send_sem=halo_send.at[l, c, 0], recv_sem=halo_recv.at[l, c, 0],
            device_id=(depth, jnp.maximum(rows - 1, 0)), device_id_type=MESH,
        )

    def halo_up(l, c):
        return pltpu.make_async_remote_copy(
            src_ref=field.at[l, c, :, pl.ds(ROWS_DEV, KR), :] if l else inc.at[c, :, pl.ds(KR, KR), :],
            dst_ref=field.at[l, c, :, pl.ds(0, KR), :],
            send_sem=halo_send.at[l, c, 1], recv_sem=halo_recv.at[l, c, 1],
            device_id=(depth, jnp.minimum(rows + 1, last)), device_id_type=MESH,
        )

    @pl.when(rows < last)
    def _():
        for c in range(COLORS):
            halo_up(0, c).start()

    expand[...] = jnp.where(
        lax.shift_right_logical(iota((NH, COLS), 1), 4) == iota((NH, COLS), 0), 1.0, 0.0
    ).astype(BF16)
    load_idx.wait()
    load_cnt.wait()
    live = []
    for g in range(ROWS_DEV // HS):
        named = (idx_in[0, g : g + 1, :] == iota((NH, NH), 0)) & (iota((NH, NH), 1) < cnt_in[0:1, g : g + 1])
        spots = lax.dot_general(
            jnp.ones((HS, NH), BF16), jnp.where(named, 1.0, 0.0).astype(BF16),
            (((1,), (1,)), ((), ())), preferred_element_type=F32,
        )
        live.append(dot(spots.astype(BF16), expand[...]))
    live = jnp.concatenate(live, axis=0) * LIGHT_SCALE

    def light_copy(l, c, dest):
        return pltpu.make_async_remote_copy(
            src_ref=lights.at[l, c], dst_ref=lights.at[l, c],
            send_sem=light_send.at[LAYERS * l + dest, c], recv_sem=light_recv.at[l, c],
            device_id=(dest, rows), device_id_type=MESH,
        )

    def meta_copy(dest):
        return pltpu.make_async_remote_copy(
            src_ref=meta.at[depth], dst_ref=meta.at[depth],
            send_sem=meta_send.at[dest], recv_sem=meta_recv.at[depth],
            device_id=(jnp.minimum(dest, planes - 1), rows), device_id_type=MESH,
        )

    load_ct.wait()
    load_rt.wait()
    load_sil.wait()
    taps[...] = jnp.zeros_like(taps)
    for c in range(COLORS):
        taps[2 * c : 2 * c + 2, 0 : 2 * KC + 1] = ct_in[0, c].astype(F32)
        taps[8 + 2 * c : 10 + 2 * c, 0 : 2 * KR + 1] = rt_in[0, c].astype(F32)
    flip = jnp.where(iota((128, 128), 0) + iota((128, 128), 1) == 2 * KC + 1, 1.0, 0.0).astype(BF16)
    turned = dot(taps[0:8, :].astype(BF16), flip)
    plain = taps[8:16, :]
    shifted = pltpu.roll(plain, 64, 1)
    for c in range(COLORS):
        re, im = slice(2 * c, 2 * c + 1), slice(2 * c + 1, 2 * c + 2)
        taps[8 + 2 * c : 9 + 2 * c, :] = plain[re] - shifted[im]
        taps[9 + 2 * c : 10 + 2 * c, :] = plain[im] + shifted[re]
    taps[0:8, :] = turned
    meta[depth] = jnp.zeros((ROWS_DEV + HS, 128), BF16)
    meta[depth, 0:ROWS_DEV, 0:NH] = sil_in[0].astype(F32).astype(BF16)
    meta[depth, ROWS_DEV:, :] = taps[...].astype(BF16)
    for dest in range(LAYERS - 1, 0, -1):
        @pl.when(depth < dest)
        def _():
            meta_copy(dest).start()

    for c in range(COLORS):
        load_light[c].wait()
    for c in range(COLORS):
        lights[depth, c] = (light_in[c] * live).astype(BF16)

    @pl.when(depth == 0)
    def _():
        for c in range(COLORS):
            light_copy(0, c, 3).start()
            light_copy(0, c, 1).start()

    @pl.when(depth == 1)
    def _():
        for c in range(COLORS):
            light_copy(1, c, 2).start()

    @pl.when(depth == 2)
    def _():
        for c in range(COLORS):
            light_copy(2, c, 3).start()

    @pl.when(rows > 0)
    def _():
        pl.semaphore_wait(ready, 1)
        for c in range(COLORS):
            halo_down(0, c).start()

    before = (depth, jnp.maximum(rows - 1, 0))
    after = (depth, jnp.minimum(rows + 1, last))

    def broad_copy(c, side, height):
        to = 2 * KR + ROWS_DEV if side == 0 else 2 * KR - height
        start = 2 * KR if side == 0 else 2 * KR + ROWS_DEV - height
        return pltpu.make_async_remote_copy(
            src_ref=broad.at[c, :, pl.ds(start, height), :], dst_ref=broad.at[c, :, pl.ds(to, height), :],
            send_sem=broad_send.at[c, side], recv_sem=broad_recv.at[c, side],
            device_id=(before, after)[side], device_id_type=MESH,
        )

    def edge_copies(side):
        start = 0 if side == 0 else ROWS_DEV - HS
        pairs = [(lights.at[2, c, pl.ds(start, HS), :], edge_light.at[1 - side, c]) for c in range(COLORS)]
        pairs.append((meta.at[2, pl.ds(start, HS), :], edge_meta.at[1 - side]))
        return [
            pltpu.make_async_remote_copy(
                src_ref=src, dst_ref=dst, send_sem=edge_send.at[side, i], recv_sem=edge_recv.at[side, i],
                device_id=(before, after)[side], device_id_type=MESH,
            )
            for i, (src, dst) in enumerate(pairs)
        ]

    def from_both(up, down):
        @pl.when(rows > 0)
        def _():
            up().wait_recv()

        @pl.when(rows < last)
        def _():
            down().wait_recv()

    def to_both(down, up):
        @pl.when(rows > 0)
        def _():
            down().start()

        @pl.when(rows < last)
        def _():
            up().start()

    def sent_both(down, up):
        @pl.when(rows > 0)
        def _():
            down().wait_send()

        @pl.when(rows < last)
        def _():
            up().wait_send()

    def wait_meta(l):
        @pl.when(depth > l)
        def _():
            pltpu.make_async_remote_copy(
                src_ref=meta.at[l], dst_ref=meta.at[l], send_sem=meta_send.at[0], recv_sem=meta_recv.at[l],
                device_id=(depth, rows), device_id_type=MESH,
            ).wait_recv()

    def wait_light(l, c):
        @pl.when(depth > l)
        def _():
            light_copy(l, c, 3).wait_recv()

    def opening(edges, height):
        within = (iota((height, COLS), 1) & (HS - 1)).astype(F32)
        return jnp.where(within < dot(edges, expand[...]), 1.0, 0.0)

    def narrow_rows(l):
        for c in range(COLORS):
            for comp in range(2):
                line = meta[l, ROWS_DEV:, :].astype(F32)[8 + 2 * c + comp : 9 + 2 * c + comp]
                row_mat[c, ROWS_DEV * comp : ROWS_DEV * (comp + 1), :] = pltpu.roll(
                    jnp.broadcast_to(line, (ROWS_DEV, 128)), 0, 1, stride=1, stride_axis=0
                ).astype(BF16)
        clear[...] = opening(meta[l, 0:ROWS_DEV, 0:NH], ROWS_DEV)

    def wide_rows(l):
        for c in range(COLORS):
            for comp in range(2):
                line = meta[l, ROWS_DEV:, :].astype(F32)[8 + 2 * c + comp : 9 + 2 * c + comp]
                first = iota((1, 128), 1) < 64
                none = jnp.zeros((1, 128), F32)
                line = jnp.concatenate([jnp.where(first, line, 0.0), none], axis=1) + pltpu.roll(
                    jnp.concatenate([jnp.where(first, 0.0, line), none], axis=1), 32, 1
                )
                row_wide[c, EXT * comp : EXT * (comp + 1), :] = pltpu.roll(
                    jnp.broadcast_to(line, (EXT, 256)), 0, 1, stride=1, stride_axis=0
                )[:, 0 : 2 * (EXT + ROWS_DEV)].astype(BF16)

    def columns(l, slot):
        lines = meta[l, ROWS_DEV:, :].astype(F32)
        below = iota((128, 128), 0) > iota((128, 128), 1)
        above = iota((128, 128), 0) < iota((128, 128), 1)
        for c in range(COLORS):
            turn = [
                pltpu.roll(
                    jnp.broadcast_to(lines[2 * c + comp : 2 * c + comp + 1], (128, 128)),
                    0, 1, stride=1, stride_axis=0,
                )
                for comp in range(2)
            ]
            for half, inside in enumerate((below, above)):
                real = jnp.where(inside, turn[0], 0.0)
                imag = jnp.where(inside, turn[1], 0.0)
                top, low = 128 * half, 256 + 128 * half
                col_mat[slot, c, top : top + 128, 0:128] = real.astype(BF16)
                col_mat[slot, c, top : top + 128, 128:256] = imag.astype(BF16)
                col_mat[slot, c, low : low + 128, 0:128] = (-imag).astype(BF16)
                col_mat[slot, c, low : low + 128, 128:256] = real.astype(BF16)

    def transform(c, value, spot):
        half_done = dot(left_in[...], value).astype(BF16)
        for t in range(TILES):
            here = slice(128 * t, 128 * (t + 1))
            mixed[spot, c, ROWS_DEV * t : ROWS_DEV * (t + 1), 0:128] = half_done[0:ROWS_DEV, here]
            mixed[spot, c, ROWS_DEV * t : ROWS_DEV * (t + 1), 128:256] = half_done[ROWS_DEV:, here]
        return dot(mixed[spot, c], right_in[...])

    def keep_transform(c, value, spot, ref, start):
        done = transform(c, value, spot)
        for t in range(TILES):
            for comp in range(2):
                ref[c, comp, start : start + ROWS_DEV, 128 * t : 128 * (t + 1)] = done[
                    ROWS_DEV * t : ROWS_DEV * (t + 1), 128 * comp : 128 * (comp + 1)
                ]

    def propagate(value, mat, pad, slot, c, height):
        rowed = dot(mat[c], value)
        wide = jnp.concatenate([rowed, jnp.zeros((2 * height, 128), F32)], axis=1)
        pad[c] = pltpu.roll(wide, 64, 1).astype(BF16)
        windows = jnp.concatenate(
            [
                jnp.concatenate(
                    [pad[c, 0:height, 128 * t : 128 * t + 256], pad[c, height:, 128 * t : 128 * t + 256]], axis=1
                )
                for t in range(TILES)
            ],
            axis=0,
        )
        return dot(windows, col_mat[slot, c])

    def pieces():
        for t in range(TILES):
            for comp in range(2):
                yield t, comp, slice(128 * t, 128 * (t + 1)), slice(128 * comp, 128 * (comp + 1))

    def step(l, c, value, store):
        done = transform(c, lights[l, c], 0)
        columned = propagate(value, row_mat, vpad, 0, c, ROWS_DEV)
        for t, comp, here, side in pieces():
            band = slice(ROWS_DEV * t, ROWS_DEV * (t + 1))
            store(comp, here, (columned[band, side] * clear[:, here] + done[band, side]).astype(BF16))

    @pl.when(depth == 1)
    def _():
        for c in range(COLORS):
            light_copy(0, c, 2).wait_recv()
            light_copy(0, c, 2).start()

    @pl.when(depth == 2)
    def _():
        for c in range(COLORS):
            light_copy(1, c, 3).wait_recv()
            light_copy(1, c, 3).start()

    wait_meta(0)
    narrow_rows(0)
    columns(0, 0)

    for c in range(COLORS):
        load_inc[c].wait()
    load_left.wait()
    load_right.wait()
    for c in range(COLORS):
        @pl.when(depth > 1)
        def _():
            wait_light(0, c)

        from_both(lambda: halo_up(0, c), lambda: halo_down(0, c))

        def store(comp, here, value):
            field[1, c, comp, KR : KR + ROWS_DEV, here] = value
            out[0, c, comp, :, here] = value

        step(0, c, field[0, c].reshape(2 * EXT, COLS), store)

        @pl.when(depth > 0)
        def _():
            to_both(lambda: halo_down(1, c), lambda: halo_up(1, c))

    @pl.when(depth == 3)
    def _():
        wait_meta(2)
        for c in range(COLORS):
            wait_light(2, c)

        @pl.when(rows > 0)
        def _():
            for copy in edge_copies(0):
                copy.start()

        @pl.when(rows < last)
        def _():
            for copy in edge_copies(1):
                copy.start()

    @pl.when(depth > 0)
    def _():
        wait_meta(1)
        narrow_rows(1)
        columns(1, 0)
        for c in range(COLORS):
            @pl.when((depth == 3))
            def _():
                wait_light(1, c)

            from_both(lambda: halo_up(1, c), lambda: halo_down(1, c))

            def store(comp, here, value):
                broad[c, comp, 2 * KR : 2 * KR + ROWS_DEV, here] = value
                out[0, c, comp, :, here] = value

            step(1, c, field[1, c].reshape(2 * EXT, COLS), store)

            @pl.when(depth == 2)
            def _():
                to_both(lambda: broad_copy(c, 0, KR), lambda: broad_copy(c, 1, KR))

            @pl.when(depth == 3)
            def _():
                to_both(lambda: broad_copy(c, 0, 2 * KR), lambda: broad_copy(c, 1, 2 * KR))

    @pl.when(depth == 2)
    def _():
        narrow_rows(2)
        columns(2, 0)
        for c in range(COLORS):
            from_both(lambda: broad_copy(c, 1, KR), lambda: broad_copy(c, 0, KR))

            def store(comp, here, value):
                out[0, c, comp, :, here] = value

            step(2, c, broad[c, :, KR : KR + EXT, :].reshape(2 * EXT, COLS), store)

    @pl.when(depth == 3)
    def _():
        narrow_rows(3)
        wide_rows(2)
        columns(3, 0)
        columns(2, 1)
        for c in range(COLORS):
            keep_transform(c, lights[3, c], 0, stereo, 0)

        @pl.when(rows > 0)
        def _():
            for copy in edge_copies(1):
                copy.wait_recv()

        @pl.when(rows < last)
        def _():
            for copy in edge_copies(0):
                copy.wait_recv()

        clear_wide[...] = opening(
            jnp.concatenate([edge_meta[0], meta[2, 0:ROWS_DEV, :], edge_meta[1]], axis=0)[:, 0:NH], EXT
        )
        for c in range(COLORS):
            upper = jnp.concatenate([edge_light[0, c], lights[2, c, 0:HS, :]], axis=0)
            lower = jnp.concatenate([lights[2, c, HS:, :], edge_light[1, c]], axis=0)
            keep_transform(c, upper, 0, stereo_wide, 0)
            keep_transform(c, lower, 1, stereo_wide, ROWS_DEV)

        def finish(c):
            columned = propagate(inner[c].reshape(2 * EXT, COLS), row_mat, vpad, 0, c, ROWS_DEV)
            for t, comp, here, side in pieces():
                band = slice(ROWS_DEV * t, ROWS_DEV * (t + 1))
                value = columned[band, side] * clear[:, here] + stereo[c, comp, :, here]
                out[0, c, comp, :, here] = value.astype(BF16)

        for c in range(COLORS):
            from_both(lambda: broad_copy(c, 1, 2 * KR), lambda: broad_copy(c, 0, 2 * KR))
            columned = propagate(
                broad[c].reshape(2 * (EXT + ROWS_DEV), COLS), row_wide, vpad_wide, 1, c, EXT
            )
            for t, comp, here, side in pieces():
                band = slice(EXT * t, EXT * (t + 1))
                value = columned[band, side] * clear_wide[:, here] + stereo_wide[c, comp, :, here]
                inner[c, comp, :, here] = value.astype(BF16)
            if c > 0:
                finish(c - 1)
        finish(COLORS - 1)

    for c in range(COLORS):
        sent_both(lambda: halo_down(0, c), lambda: halo_up(0, c))

        @pl.when(depth > 0)
        def _():
            sent_both(lambda: halo_down(1, c), lambda: halo_up(1, c))

        @pl.when(depth == 2)
        def _():
            sent_both(lambda: broad_copy(c, 0, KR), lambda: broad_copy(c, 1, KR))

        @pl.when(depth == 3)
        def _():
            sent_both(lambda: broad_copy(c, 0, 2 * KR), lambda: broad_copy(c, 1, 2 * KR))

    @pl.when((depth == 3) & (rows > 0))
    def _():
        for copy in edge_copies(0):
            copy.wait_send()

    @pl.when((depth == 3) & (rows < last))
    def _():
        for copy in edge_copies(1):
            copy.wait_send()

    for dest in range(1, LAYERS):
        @pl.when(depth < dest)
        def _():
            meta_copy(dest).wait_send()

    for at, l, dest in ((0, 0, 3), (0, 0, 1), (1, 1, 2), (2, 2, 3), (2, 1, 3), (1, 0, 2)):
        @pl.when(depth == at)
        def _():
            for c in range(COLORS):
                light_copy(l, c, dest).wait_send()


def body(incident, row_taps, col_taps, hogel_light, silhouette, fill_counts, hogel_index):
    left, right = dft_constants()
    anywhere = pl.BlockSpec(memory_space=pltpu.HBM)
    dma = pltpu.SemaphoreType.DMA
    return pl.pallas_call(
        kernel,
        name="hologram",
        out_shape=jax.ShapeDtypeStruct((1,) + incident.shape, BF16),
        in_specs=[anywhere] * 9,
        out_specs=pl.BlockSpec(memory_space=pltpu.VMEM),
        scratch_shapes=[
            pltpu.VMEM((2, COLORS, 2, EXT, COLS), BF16),
            pltpu.VMEM((COLORS, 2, EXT + ROWS_DEV, COLS), BF16),
            pltpu.VMEM((COLORS, 2, EXT, COLS), BF16),
            pltpu.VMEM((LAYERS, COLORS, ROWS_DEV, COLS), BF16),
            pltpu.VMEM((2, COLORS, HS, COLS), BF16),
            pltpu.VMEM((LAYERS, ROWS_DEV + HS, 128), BF16),
            pltpu.VMEM((2, HS, 128), BF16),
            pltpu.VMEM((COLORS, ROWS_DEV, COLS), F32),
            pltpu.VMEM(row_taps.shape, BF16),
            pltpu.VMEM(col_taps.shape, BF16),
            pltpu.VMEM(silhouette.shape, jnp.int32),
            pltpu.VMEM(fill_counts.shape, jnp.int32),
            pltpu.VMEM(hogel_index.shape, jnp.int32),
            pltpu.VMEM(left.shape, BF16),
            pltpu.VMEM(right.shape, BF16),
            pltpu.VMEM((16, 128), F32),
            pltpu.VMEM((NH, COLS), BF16),
            pltpu.VMEM((COLORS, 2 * ROWS_DEV, 128), BF16),
            pltpu.VMEM((COLORS, 2 * EXT, 2 * (EXT + ROWS_DEV)), BF16),
            pltpu.VMEM((2, COLORS, 512, 256), BF16),
            pltpu.VMEM((ROWS_DEV, COLS), F32),
            pltpu.VMEM((EXT, COLS), F32),
            pltpu.VMEM((COLORS, 2, ROWS_DEV, COLS), F32),
            pltpu.VMEM((COLORS, 2, EXT, COLS), F32),
            pltpu.VMEM((COLORS, 2 * ROWS_DEV, COLS + 128), BF16),
            pltpu.VMEM((COLORS, 2 * EXT, COLS + 128), BF16),
            pltpu.VMEM((2, COLORS, ROWS_DEV * TILES, 256), BF16),
            dma((13,)),
            dma((2, COLORS, 2)),
            dma((2, COLORS, 2)),
            dma((COLORS, 2)),
            dma((COLORS, 2)),
            dma((2, COLORS + 1)),
            dma((2, COLORS + 1)),
            dma((LAYERS * LAYERS, COLORS)),
            dma((LAYERS, COLORS)),
            dma((LAYERS,)),
            dma((LAYERS,)),
            pltpu.SemaphoreType.REGULAR,
        ],
        compiler_params=pltpu.CompilerParams(
            collective_id=0, has_side_effects=True, vmem_limit_bytes=40 << 20
        ),
    )(*[
        pltpu.with_memory_space_constraint(x, pltpu.HBM)
        for x in (
            incident, row_taps, col_taps, hogel_light, silhouette, fill_counts, hogel_index,
            jnp.asarray(left), jnp.asarray(right),
        )
    ])


def solution(mesh):
    placed = (
        P(None, None, "rows", None),
        P("depth", None, None, None),
        P("depth", None, None, None),
        P("depth", None, "rows", None),
        P("depth", "rows", None),
        P("depth", "rows"),
        P("depth", "rows", None),
    )
    return jax.shard_map(
        body,
        mesh=mesh,
        in_specs=placed,
        out_specs=P("depth", None, None, "rows", None),
        check_vma=False,
    )
```

```python
import math

import jax
import jax.numpy as jnp
import ml_dtypes
import numpy as np
from jax import lax
from jax.experimental import pallas as pl
from jax.experimental.pallas import tpu as pltpu
from jax.sharding import PartitionSpec as P

HS = 16
KR = 16
KC = 63
COLORS = 3
ROWS_DEV = 32
COLS = 1024
LAYERS = 4
NH = 64
TILES = COLS // 128
EXT = ROWS_DEV + 2 * KR
TABLE_SCALE = 1.132805
LIGHT_SCALE = 1.0 / (HS * TABLE_SCALE * TABLE_SCALE)
MESH = pl.DeviceIdType.MESH
F32 = jnp.float32
BF16 = jnp.bfloat16


def dft_constants():
    counter = np.arange(HS)
    angles = (counter[:, None] * counter[None, :] % HS) * (2.0 * math.pi / HS)
    cos_tab, sin_tab = TABLE_SCALE * np.cos(angles), TABLE_SCALE * np.sin(angles)
    groups, per_block = ROWS_DEV // HS, 128 // HS
    left = np.concatenate([np.kron(np.eye(groups), cos_tab), np.kron(np.eye(groups), -sin_tab)], axis=0)
    cos_big, sin_big = np.kron(np.eye(per_block), cos_tab), np.kron(np.eye(per_block), sin_tab)
    right = np.block([[cos_big, -sin_big], [sin_big, cos_big]])
    return left.astype(ml_dtypes.bfloat16), right.astype(ml_dtypes.bfloat16)


def dot(a, b):
    return jnp.dot(a, b, preferred_element_type=F32)


def iota(shape, dim):
    return lax.broadcasted_iota(jnp.int32, shape, dim)


def kernel(
    inc, row_taps, col_taps, light, sil, counts, index, left, right, out,
    field, broad, inner, lights, edge_light, meta, edge_meta,
    light_in, rt_in, ct_in, sil_in, cnt_in, idx_in, left_in, right_in,
    taps, expand, row_mat, row_wide, col_mat, clear, clear_wide, stereo, stereo_wide, vpad, vpad_wide, mixed,
    load_sem, halo_send, halo_recv, broad_send, broad_recv, edge_send, edge_recv,
    light_send, light_recv, meta_send, meta_recv, ready,
):
    depth, rows = lax.axis_index("depth"), lax.axis_index("rows")
    last = lax.axis_size("rows") - 1
    planes = lax.axis_size("depth")

    barrier = pltpu.get_barrier_semaphore()

    @pl.when(rows > 0)
    def _():
        pl.semaphore_signal(barrier, inc=1, device_id=(depth, rows - 1), device_id_type=MESH)

    for back in range(1, LAYERS):
        @pl.when(depth >= back)
        def _():
            pl.semaphore_signal(barrier, inc=1, device_id=(depth - back, rows), device_id_type=MESH)

    loads = []
    pairs = [(inc.at[c], field.at[0, c, :, pl.ds(KR, ROWS_DEV), :]) for c in range(COLORS)]
    pairs += [(light.at[0, c], light_in.at[c]) for c in range(COLORS)]
    pairs += [(index, idx_in), (counts, cnt_in), (col_taps, ct_in), (row_taps, rt_in), (sil, sil_in)]
    pairs += [(left, left_in), (right, right_in)]
    for i, (src, dst) in enumerate(pairs):
        copy = pltpu.make_async_copy(src, dst, load_sem.at[i])
        copy.start()
        loads.append(copy)
    load_inc, load_light = loads[:COLORS], loads[COLORS : 2 * COLORS]
    load_idx, load_cnt, load_ct, load_rt, load_sil, load_left, load_right = loads[2 * COLORS :]

    @pl.when(rows == 0)
    def _():
        field[:, :, :, 0:KR, :] = jnp.zeros((2, COLORS, 2, KR, COLS), BF16)
        broad[:, :, 0 : 2 * KR, :] = jnp.zeros((COLORS, 2, 2 * KR, COLS), BF16)
        edge_light[0] = jnp.zeros((COLORS, HS, COLS), BF16)
        edge_meta[0] = jnp.zeros((HS, 128), BF16)

    @pl.when(rows == last)
    def _():
        field[:, :, :, KR + ROWS_DEV :, :] = jnp.zeros((2, COLORS, 2, KR, COLS), BF16)
        broad[:, :, 2 * KR + ROWS_DEV :, :] = jnp.zeros((COLORS, 2, 2 * KR, COLS), BF16)
        edge_light[1] = jnp.zeros((COLORS, HS, COLS), BF16)
        edge_meta[1] = jnp.zeros((HS, 128), BF16)

    def halo_down(l, c):
        return pltpu.make_async_remote_copy(
            src_ref=field.at[l, c, :, pl.ds(KR, KR), :] if l else inc.at[c, :, pl.ds(0, KR), :],
            dst_ref=field.at[l, c, :, pl.ds(KR + ROWS_DEV, KR), :],
            send_sem=halo_send.at[l, c, 0], recv_sem=halo_recv.at[l, c, 0],
            device_id=(depth, jnp.maximum(rows - 1, 0)), device_id_type=MESH,
        )

    def halo_up(l, c):
        return pltpu.make_async_remote_copy(
            src_ref=field.at[l, c, :, pl.ds(ROWS_DEV, KR), :] if l else inc.at[c, :, pl.ds(KR, KR), :],
            dst_ref=field.at[l, c, :, pl.ds(0, KR), :],
            send_sem=halo_send.at[l, c, 1], recv_sem=halo_recv.at[l, c, 1],
            device_id=(depth, jnp.minimum(rows + 1, last)), device_id_type=MESH,
        )

    greetings = planes - 1 - depth + jnp.where(rows < last, 1, 0)

    def greeted():
        @pl.when(greetings > 0)
        def _():
            pl.semaphore_wait(barrier, greetings)

        @pl.when(rows < last)
        def _():
            pl.semaphore_signal(ready, inc=1, device_id=(depth, rows + 1), device_id_type=MESH)
            for c in range(COLORS):
                halo_up(0, c).start()

    @pl.when(depth == 3)
    def _():
        greeted()

    expand[...] = jnp.where(
        lax.shift_right_logical(iota((NH, COLS), 1), 4) == iota((NH, COLS), 0), 1.0, 0.0
    ).astype(BF16)
    load_idx.wait()
    load_cnt.wait()
    live = []
    for g in range(ROWS_DEV // HS):
        named = (idx_in[0, g : g + 1, :] == iota((NH, NH), 0)) & (iota((NH, NH), 1) < cnt_in[0:1, g : g + 1])
        spots = lax.dot_general(
            jnp.ones((HS, NH), BF16), jnp.where(named, 1.0, 0.0).astype(BF16),
            (((1,), (1,)), ((), ())), preferred_element_type=F32,
        )
        live.append(dot(spots.astype(BF16), expand[...]))
    live = jnp.concatenate(live, axis=0) * LIGHT_SCALE

    def light_copy(l, c, dest):
        return pltpu.make_async_remote_copy(
            src_ref=lights.at[l, c], dst_ref=lights.at[l, c],
            send_sem=light_send.at[LAYERS * l + dest, c], recv_sem=light_recv.at[l, c],
            device_id=(dest, rows), device_id_type=MESH,
        )

    def meta_copy(dest):
        return pltpu.make_async_remote_copy(
            src_ref=meta.at[depth], dst_ref=meta.at[depth],
            send_sem=meta_send.at[dest], recv_sem=meta_recv.at[depth],
            device_id=(jnp.minimum(dest, planes - 1), rows), device_id_type=MESH,
        )

    load_ct.wait()
    load_rt.wait()
    load_sil.wait()
    taps[...] = jnp.zeros_like(taps)
    for c in range(COLORS):
        taps[2 * c : 2 * c + 2, 0 : 2 * KC + 1] = ct_in[0, c].astype(F32)
        taps[8 + 2 * c : 10 + 2 * c, 0 : 2 * KR + 1] = rt_in[0, c].astype(F32)
    flip = jnp.where(iota((128, 128), 0) + iota((128, 128), 1) == 2 * KC + 1, 1.0, 0.0).astype(BF16)
    turned = dot(taps[0:8, :].astype(BF16), flip)
    plain = taps[8:16, :]
    shifted = pltpu.roll(plain, 64, 1)
    for c in range(COLORS):
        re, im = slice(2 * c, 2 * c + 1), slice(2 * c + 1, 2 * c + 2)
        taps[8 + 2 * c : 9 + 2 * c, :] = plain[re] - shifted[im]
        taps[9 + 2 * c : 10 + 2 * c, :] = plain[im] + shifted[re]
    taps[0:8, :] = turned
    meta[depth] = jnp.zeros((ROWS_DEV + HS, 128), BF16)
    meta[depth, 0:ROWS_DEV, 0:NH] = sil_in[0].astype(F32).astype(BF16)
    meta[depth, ROWS_DEV:, :] = taps[...].astype(BF16)
    for c in range(COLORS):
        load_light[c].wait()
    for c in range(COLORS):
        lights[depth, c] = (light_in[c] * live).astype(BF16)

    @pl.when(depth < 3)
    def _():
        greeted()

    for dest in range(LAYERS - 1, 0, -1):
        @pl.when(depth < dest)
        def _():
            meta_copy(dest).start()

    @pl.when(depth == 0)
    def _():
        for c in range(COLORS):
            light_copy(0, c, 3).start()
            light_copy(0, c, 1).start()

    @pl.when(depth == 1)
    def _():
        for c in range(COLORS):
            light_copy(1, c, 2).start()

    @pl.when(depth == 2)
    def _():
        for c in range(COLORS):
            light_copy(2, c, 3).start()

    @pl.when(rows > 0)
    def _():
        pl.semaphore_wait(ready, 1)
        for c in range(COLORS):
            halo_down(0, c).start()

    before = (depth, jnp.maximum(rows - 1, 0))
    after = (depth, jnp.minimum(rows + 1, last))

    def broad_copy(c, side, height):
        to = 2 * KR + ROWS_DEV if side == 0 else 2 * KR - height
        start = 2 * KR if side == 0 else 2 * KR + ROWS_DEV - height
        return pltpu.make_async_remote_copy(
            src_ref=broad.at[c, :, pl.ds(start, height), :], dst_ref=broad.at[c, :, pl.ds(to, height), :],
            send_sem=broad_send.at[c, side], recv_sem=broad_recv.at[c, side],
            device_id=(before, after)[side], device_id_type=MESH,
        )

    def edge_copies(side):
        start = 0 if side == 0 else ROWS_DEV - HS
        pairs = [(lights.at[2, c, pl.ds(start, HS), :], edge_light.at[1 - side, c]) for c in range(COLORS)]
        pairs.append((meta.at[2, pl.ds(start, HS), :], edge_meta.at[1 - side]))
        return [
            pltpu.make_async_remote_copy(
                src_ref=src, dst_ref=dst, send_sem=edge_send.at[side, i], recv_sem=edge_recv.at[side, i],
                device_id=(before, after)[side], device_id_type=MESH,
            )
            for i, (src, dst) in enumerate(pairs)
        ]

    def from_both(up, down):
        @pl.when(rows > 0)
        def _():
            up().wait_recv()

        @pl.when(rows < last)
        def _():
            down().wait_recv()

    def to_both(down, up):
        @pl.when(rows > 0)
        def _():
            down().start()

        @pl.when(rows < last)
        def _():
            up().start()

    def sent_both(down, up):
        @pl.when(rows > 0)
        def _():
            down().wait_send()

        @pl.when(rows < last)
        def _():
            up().wait_send()

    def wait_meta(l):
        @pl.when(depth > l)
        def _():
            pltpu.make_async_remote_copy(
                src_ref=meta.at[l], dst_ref=meta.at[l], send_sem=meta_send.at[0], recv_sem=meta_recv.at[l],
                device_id=(depth, rows), device_id_type=MESH,
            ).wait_recv()

    def wait_light(l, c):
        @pl.when(depth > l)
        def _():
            light_copy(l, c, 3).wait_recv()

    def opening(edges, height):
        within = (iota((height, COLS), 1) & (HS - 1)).astype(F32)
        return jnp.where(within < dot(edges, expand[...]), 1.0, 0.0)

    def narrow_rows(l, slot):
        for c in range(COLORS):
            for comp in range(2):
                line = meta[l, ROWS_DEV:, :].astype(F32)[8 + 2 * c + comp : 9 + 2 * c + comp]
                row_mat[slot, c, ROWS_DEV * comp : ROWS_DEV * (comp + 1), :] = pltpu.roll(
                    jnp.broadcast_to(line, (ROWS_DEV, 128)), 0, 1, stride=1, stride_axis=0
                ).astype(BF16)
        clear[slot] = opening(meta[l, 0:ROWS_DEV, 0:NH], ROWS_DEV)

    def wide_rows(l):
        for c in range(COLORS):
            for comp in range(2):
                line = meta[l, ROWS_DEV:, :].astype(F32)[8 + 2 * c + comp : 9 + 2 * c + comp]
                first = iota((1, 128), 1) < 64
                none = jnp.zeros((1, 128), F32)
                line = jnp.concatenate([jnp.where(first, line, 0.0), none], axis=1) + pltpu.roll(
                    jnp.concatenate([jnp.where(first, 0.0, line), none], axis=1), 32, 1
                )
                row_wide[c, EXT * comp : EXT * (comp + 1), :] = pltpu.roll(
                    jnp.broadcast_to(line, (EXT, 256)), 0, 1, stride=1, stride_axis=0
                )[:, 0 : 2 * (EXT + ROWS_DEV)].astype(BF16)

    def columns(l, slot):
        lines = meta[l, ROWS_DEV:, :].astype(F32)
        below = iota((128, 128), 0) > iota((128, 128), 1)
        above = iota((128, 128), 0) < iota((128, 128), 1)
        for c in range(COLORS):
            turn = [
                pltpu.roll(
                    jnp.broadcast_to(lines[2 * c + comp : 2 * c + comp + 1], (128, 128)),
                    0, 1, stride=1, stride_axis=0,
                )
                for comp in range(2)
            ]
            for half, inside in enumerate((below, above)):
                real = jnp.where(inside, turn[0], 0.0)
                imag = jnp.where(inside, turn[1], 0.0)
                top, low = 128 * half, 256 + 128 * half
                col_mat[slot, c, top : top + 128, 0:128] = real.astype(BF16)
                col_mat[slot, c, top : top + 128, 128:256] = imag.astype(BF16)
                col_mat[slot, c, low : low + 128, 0:128] = (-imag).astype(BF16)
                col_mat[slot, c, low : low + 128, 128:256] = real.astype(BF16)

    def transform(c, value, spot):
        half_done = dot(left_in[...], value).astype(BF16)
        for t in range(TILES):
            here = slice(128 * t, 128 * (t + 1))
            mixed[spot, c, ROWS_DEV * t : ROWS_DEV * (t + 1), 0:128] = half_done[0:ROWS_DEV, here]
            mixed[spot, c, ROWS_DEV * t : ROWS_DEV * (t + 1), 128:256] = half_done[ROWS_DEV:, here]
        return dot(mixed[spot, c], right_in[...])

    def keep_transform(c, value, spot, ref, start):
        done = transform(c, value, spot)
        for t in range(TILES):
            for comp in range(2):
                ref[c, comp, start : start + ROWS_DEV, 128 * t : 128 * (t + 1)] = done[
                    ROWS_DEV * t : ROWS_DEV * (t + 1), 128 * comp : 128 * (comp + 1)
                ]

    def propagate(value, mat, pad, slot, c, height):
        rowed = dot(mat[c], value)
        wide = jnp.concatenate([rowed, jnp.zeros((2 * height, 128), F32)], axis=1)
        pad[c] = pltpu.roll(wide, 64, 1).astype(BF16)
        windows = jnp.concatenate(
            [
                jnp.concatenate(
                    [pad[c, 0:height, 128 * t : 128 * t + 256], pad[c, height:, 128 * t : 128 * t + 256]], axis=1
                )
                for t in range(TILES)
            ],
            axis=0,
        )
        return dot(windows, col_mat[slot, c])

    def pieces():
        for t in range(TILES):
            for comp in range(2):
                yield t, comp, slice(128 * t, 128 * (t + 1)), slice(128 * comp, 128 * (comp + 1))

    def step(l, c, value, store):
        done = transform(c, lights[l, c], 0)
        columned = propagate(value, row_mat.at[0], vpad, 0, c, ROWS_DEV)
        for t, comp, here, side in pieces():
            band = slice(ROWS_DEV * t, ROWS_DEV * (t + 1))
            store(comp, here, (columned[band, side] * clear[0, :, here] + done[band, side]).astype(BF16))

    def step_on_kept(c, value, store, slot, col_slot):
        columned = propagate(value, row_mat.at[slot], vpad, col_slot, c, ROWS_DEV)
        for t, comp, here, side in pieces():
            band = slice(ROWS_DEV * t, ROWS_DEV * (t + 1))
            value = columned[band, side] * clear[slot, :, here] + stereo[c, comp, :, here]
            store(comp, here, value.astype(BF16))

    @pl.when(depth == 1)
    def _():
        for c in range(COLORS):
            light_copy(0, c, 2).wait_recv()
            light_copy(0, c, 2).start()

    @pl.when(depth == 2)
    def _():
        for c in range(COLORS):
            light_copy(1, c, 3).wait_recv()
            light_copy(1, c, 3).start()

    wait_meta(0)
    narrow_rows(0, 0)
    columns(0, 0)

    for c in range(COLORS):
        load_inc[c].wait()
    load_left.wait()
    load_right.wait()
    eager = lax.rem(rows, 16) == 0

    @pl.when(eager)
    def _():
        for c in range(COLORS):
            @pl.when(depth > 1)
            def _():
                wait_light(0, c)

            keep_transform(c, lights[0, c], 0, stereo, 0)

    for c in range(COLORS):
        @pl.when((depth > 1) & (lax.rem(rows, 16) > 0))
        def _():
            wait_light(0, c)

        from_both(lambda: halo_up(0, c), lambda: halo_down(0, c))

        def store(comp, here, value):
            field[1, c, comp, KR : KR + ROWS_DEV, here] = value
            out[0, c, comp, :, here] = value

        @pl.when(eager)
        def _():
            step_on_kept(c, field[0, c].reshape(2 * EXT, COLS), store, 0, 0)

        @pl.when(lax.rem(rows, 16) > 0)
        def _():
            step(0, c, field[0, c].reshape(2 * EXT, COLS), store)

        @pl.when(depth > 0)
        def _():
            to_both(lambda: halo_down(1, c), lambda: halo_up(1, c))

    @pl.when(depth == 3)
    def _():
        wait_meta(2)
        for c in range(COLORS):
            wait_light(2, c)

        @pl.when(rows > 0)
        def _():
            for copy in edge_copies(0):
                copy.start()

        @pl.when(rows < last)
        def _():
            for copy in edge_copies(1):
                copy.start()

    def prepare_last():
        @pl.when(depth == 2)
        def _():
            narrow_rows(2, 1)
            columns(2, 1)
            for c in range(COLORS):
                keep_transform(c, lights[2, c], 0, stereo, 0)

        @pl.when(depth == 3)
        def _():
            narrow_rows(3, 1)
            wide_rows(2)
            columns(3, 2)
            columns(2, 1)
            for c in range(COLORS):
                keep_transform(c, lights[3, c], 0, stereo, 0)

    @pl.when(eager)
    def _():
        prepare_last()

    @pl.when(depth > 0)
    def _():
        wait_meta(1)
        narrow_rows(1, 0)
        columns(1, 0)
        for c in range(COLORS):
            @pl.when((depth == 3))
            def _():
                wait_light(1, c)

            from_both(lambda: halo_up(1, c), lambda: halo_down(1, c))

            def store(comp, here, value):
                broad[c, comp, 2 * KR : 2 * KR + ROWS_DEV, here] = value
                out[0, c, comp, :, here] = value

            step(1, c, field[1, c].reshape(2 * EXT, COLS), store)

            @pl.when(depth == 2)
            def _():
                to_both(lambda: broad_copy(c, 0, KR), lambda: broad_copy(c, 1, KR))

            @pl.when(depth == 3)
            def _():
                to_both(lambda: broad_copy(c, 0, 2 * KR), lambda: broad_copy(c, 1, 2 * KR))

    @pl.when(lax.rem(rows, 16) > 0)
    def _():
        prepare_last()

    @pl.when(depth == 2)
    def _():
        for c in range(COLORS):
            from_both(lambda: broad_copy(c, 1, KR), lambda: broad_copy(c, 0, KR))

            def store(comp, here, value):
                out[0, c, comp, :, here] = value

            step_on_kept(c, broad[c, :, KR : KR + EXT, :].reshape(2 * EXT, COLS), store, 1, 1)

    @pl.when(depth == 3)
    def _():
        @pl.when(rows > 0)
        def _():
            for copy in edge_copies(1):
                copy.wait_recv()

        @pl.when(rows < last)
        def _():
            for copy in edge_copies(0):
                copy.wait_recv()

        clear_wide[...] = opening(
            jnp.concatenate([edge_meta[0], meta[2, 0:ROWS_DEV, :], edge_meta[1]], axis=0)[:, 0:NH], EXT
        )
        for c in range(COLORS):
            upper = jnp.concatenate([edge_light[0, c], lights[2, c, 0:HS, :]], axis=0)
            lower = jnp.concatenate([lights[2, c, HS:, :], edge_light[1, c]], axis=0)
            keep_transform(c, upper, 0, stereo_wide, 0)
            keep_transform(c, lower, 1, stereo_wide, ROWS_DEV)

        def finish(c):
            def store(comp, here, value):
                out[0, c, comp, :, here] = value

            step_on_kept(c, inner[c].reshape(2 * EXT, COLS), store, 1, 2)

        for c in range(COLORS):
            from_both(lambda: broad_copy(c, 1, 2 * KR), lambda: broad_copy(c, 0, 2 * KR))
            columned = propagate(
                broad[c].reshape(2 * (EXT + ROWS_DEV), COLS), row_wide, vpad_wide, 1, c, EXT
            )
            for t, comp, here, side in pieces():
                band = slice(EXT * t, EXT * (t + 1))
                value = columned[band, side] * clear_wide[:, here] + stereo_wide[c, comp, :, here]
                inner[c, comp, :, here] = value.astype(BF16)
            if c > 0:
                finish(c - 1)
        finish(COLORS - 1)

    for c in range(COLORS):
        sent_both(lambda: halo_down(0, c), lambda: halo_up(0, c))

        @pl.when(depth > 0)
        def _():
            sent_both(lambda: halo_down(1, c), lambda: halo_up(1, c))

        @pl.when(depth == 2)
        def _():
            sent_both(lambda: broad_copy(c, 0, KR), lambda: broad_copy(c, 1, KR))

        @pl.when(depth == 3)
        def _():
            sent_both(lambda: broad_copy(c, 0, 2 * KR), lambda: broad_copy(c, 1, 2 * KR))

    @pl.when((depth == 3) & (rows > 0))
    def _():
        for copy in edge_copies(0):
            copy.wait_send()

    @pl.when((depth == 3) & (rows < last))
    def _():
        for copy in edge_copies(1):
            copy.wait_send()

    for dest in range(1, LAYERS):
        @pl.when(depth < dest)
        def _():
            meta_copy(dest).wait_send()

    for at, l, dest in ((0, 0, 3), (0, 0, 1), (1, 1, 2), (2, 2, 3), (2, 1, 3), (1, 0, 2)):
        @pl.when(depth == at)
        def _():
            for c in range(COLORS):
                light_copy(l, c, dest).wait_send()


def body(incident, row_taps, col_taps, hogel_light, silhouette, fill_counts, hogel_index):
    left, right = dft_constants()
    anywhere = pl.BlockSpec(memory_space=pltpu.HBM)
    dma = pltpu.SemaphoreType.DMA
    return pl.pallas_call(
        kernel,
        name="hologram",
        out_shape=jax.ShapeDtypeStruct((1,) + incident.shape, BF16),
        in_specs=[anywhere] * 9,
        out_specs=pl.BlockSpec(memory_space=pltpu.VMEM),
        scratch_shapes=[
            pltpu.VMEM((2, COLORS, 2, EXT, COLS), BF16),
            pltpu.VMEM((COLORS, 2, EXT + ROWS_DEV, COLS), BF16),
            pltpu.VMEM((COLORS, 2, EXT, COLS), BF16),
            pltpu.VMEM((LAYERS, COLORS, ROWS_DEV, COLS), BF16),
            pltpu.VMEM((2, COLORS, HS, COLS), BF16),
            pltpu.VMEM((LAYERS, ROWS_DEV + HS, 128), BF16),
            pltpu.VMEM((2, HS, 128), BF16),
            pltpu.VMEM((COLORS, ROWS_DEV, COLS), F32),
            pltpu.VMEM(row_taps.shape, BF16),
            pltpu.VMEM(col_taps.shape, BF16),
            pltpu.VMEM(silhouette.shape, jnp.int32),
            pltpu.VMEM(fill_counts.shape, jnp.int32),
            pltpu.VMEM(hogel_index.shape, jnp.int32),
            pltpu.VMEM(left.shape, BF16),
            pltpu.VMEM(right.shape, BF16),
            pltpu.VMEM((16, 128), F32),
            pltpu.VMEM((NH, COLS), BF16),
            pltpu.VMEM((2, COLORS, 2 * ROWS_DEV, 128), BF16),
            pltpu.VMEM((COLORS, 2 * EXT, 2 * (EXT + ROWS_DEV)), BF16),
            pltpu.VMEM((3, COLORS, 512, 256), BF16),
            pltpu.VMEM((2, ROWS_DEV, COLS), F32),
            pltpu.VMEM((EXT, COLS), F32),
            pltpu.VMEM((COLORS, 2, ROWS_DEV, COLS), F32),
            pltpu.VMEM((COLORS, 2, EXT, COLS), F32),
            pltpu.VMEM((COLORS, 2 * ROWS_DEV, COLS + 128), BF16),
            pltpu.VMEM((COLORS, 2 * EXT, COLS + 128), BF16),
            pltpu.VMEM((2, COLORS, ROWS_DEV * TILES, 256), BF16),
            dma((13,)),
            dma((2, COLORS, 2)),
            dma((2, COLORS, 2)),
            dma((COLORS, 2)),
            dma((COLORS, 2)),
            dma((2, COLORS + 1)),
            dma((2, COLORS + 1)),
            dma((LAYERS * LAYERS, COLORS)),
            dma((LAYERS, COLORS)),
            dma((LAYERS,)),
            dma((LAYERS,)),
            pltpu.SemaphoreType.REGULAR,
        ],
        compiler_params=pltpu.CompilerParams(
            collective_id=0, has_side_effects=True, vmem_limit_bytes=40 << 20
        ),
    )(*[
        pltpu.with_memory_space_constraint(x, pltpu.HBM)
        for x in (
            incident, row_taps, col_taps, hogel_light, silhouette, fill_counts, hogel_index,
            jnp.asarray(left), jnp.asarray(right),
        )
    ])


def solution(mesh):
    placed = (
        P(None, None, "rows", None),
        P("depth", None, None, None),
        P("depth", None, None, None),
        P("depth", None, "rows", None),
        P("depth", "rows", None),
        P("depth", "rows"),
        P("depth", "rows", None),
    )
    return jax.shard_map(
        body,
        mesh=mesh,
        in_specs=placed,
        out_specs=P("depth", None, None, "rows", None),
        check_vma=False,
    )
```

```python
import math

import jax
import jax.numpy as jnp
import ml_dtypes
import numpy as np
from jax import lax
from jax.experimental import pallas as pl
from jax.experimental.pallas import tpu as pltpu
from jax.sharding import PartitionSpec as P

HS = 16
KR = 16
KC = 63
COLORS = 3
ROWS_DEV = 32
COLS = 1024
LAYERS = 4
NH = 64
TILES = COLS // 128
EXT = ROWS_DEV + 2 * KR
TABLE_SCALE = 1.132805
LIGHT_SCALE = 1.0 / (HS * TABLE_SCALE * TABLE_SCALE)
MESH = pl.DeviceIdType.MESH
F32 = jnp.float32
BF16 = jnp.bfloat16


def dft_constants():
    counter = np.arange(HS)
    angles = (counter[:, None] * counter[None, :] % HS) * (2.0 * math.pi / HS)
    cos_tab, sin_tab = TABLE_SCALE * np.cos(angles), TABLE_SCALE * np.sin(angles)
    groups, per_block = ROWS_DEV // HS, 128 // HS
    left = np.concatenate([np.kron(np.eye(groups), cos_tab), np.kron(np.eye(groups), -sin_tab)], axis=0)
    cos_big, sin_big = np.kron(np.eye(per_block), cos_tab), np.kron(np.eye(per_block), sin_tab)
    right = np.block([[cos_big, -sin_big], [sin_big, cos_big]])
    return left.astype(ml_dtypes.bfloat16), right.astype(ml_dtypes.bfloat16)


def dot(a, b):
    return jnp.dot(a, b, preferred_element_type=F32)


def iota(shape, dim):
    return lax.broadcasted_iota(jnp.int32, shape, dim)


def kernel(
    inc, row_taps, col_taps, light, sil, counts, index, left, right, out,
    field, broad, inner, lights, edge_light, meta, edge_meta,
    light_in, rt_in, ct_in, sil_in, cnt_in, idx_in, left_in, right_in,
    taps, expand, row_mat, row_wide, col_mat, clear, clear_wide, stereo, stereo_wide, vpad, vpad_wide, mixed,
    load_sem, halo_send, halo_recv, broad_send, broad_recv, edge_send, edge_recv,
    light_send, light_recv, meta_send, meta_recv, ready,
):
    depth, rows = lax.axis_index("depth"), lax.axis_index("rows")
    last = lax.axis_size("rows") - 1
    planes = lax.axis_size("depth")

    barrier = pltpu.get_barrier_semaphore()

    @pl.when(rows > 0)
    def _():
        pl.semaphore_signal(barrier, inc=1, device_id=(depth, rows - 1), device_id_type=MESH)

    for back in range(1, LAYERS):
        @pl.when(depth >= back)
        def _():
            pl.semaphore_signal(barrier, inc=1, device_id=(depth - back, rows), device_id_type=MESH)

    def halo_down(l, c):
        return pltpu.make_async_remote_copy(
            src_ref=field.at[l, c, :, pl.ds(KR, KR), :] if l else inc.at[c, :, pl.ds(0, KR), :],
            dst_ref=field.at[l, c, :, pl.ds(KR + ROWS_DEV, KR), :],
            send_sem=halo_send.at[l, c, 0], recv_sem=halo_recv.at[l, c, 0],
            device_id=(depth, jnp.maximum(rows - 1, 0)), device_id_type=MESH,
        )

    def halo_up(l, c):
        return pltpu.make_async_remote_copy(
            src_ref=field.at[l, c, :, pl.ds(ROWS_DEV, KR), :] if l else inc.at[c, :, pl.ds(KR, KR), :],
            dst_ref=field.at[l, c, :, pl.ds(0, KR), :],
            send_sem=halo_send.at[l, c, 1], recv_sem=halo_recv.at[l, c, 1],
            device_id=(depth, jnp.minimum(rows + 1, last)), device_id_type=MESH,
        )

    greetings = planes - 1 - depth + jnp.where(rows < last, 1, 0)

    def greeted():
        @pl.when(greetings > 0)
        def _():
            pl.semaphore_wait(barrier, greetings)

        @pl.when(rows < last)
        def _():
            pl.semaphore_signal(ready, inc=1, device_id=(depth, rows + 1), device_id_type=MESH)
            for c in range(COLORS):
                halo_up(0, c).start()

    @pl.when(depth == 3)
    def _():
        greeted()

    loads = []
    pairs = [(inc.at[c], field.at[0, c, :, pl.ds(KR, ROWS_DEV), :]) for c in range(COLORS)]
    pairs += [(light.at[0, c], light_in.at[c]) for c in range(COLORS)]
    pairs += [(index, idx_in), (counts, cnt_in), (col_taps, ct_in), (row_taps, rt_in), (sil, sil_in)]
    pairs += [(left, left_in), (right, right_in)]
    for i, (src, dst) in enumerate(pairs):
        copy = pltpu.make_async_copy(src, dst, load_sem.at[i])
        copy.start()
        loads.append(copy)
    load_inc, load_light = loads[:COLORS], loads[COLORS : 2 * COLORS]
    load_idx, load_cnt, load_ct, load_rt, load_sil, load_left, load_right = loads[2 * COLORS :]

    @pl.when(rows == 0)
    def _():
        field[:, :, :, 0:KR, :] = jnp.zeros((2, COLORS, 2, KR, COLS), BF16)
        broad[:, :, 0 : 2 * KR, :] = jnp.zeros((COLORS, 2, 2 * KR, COLS), BF16)
        edge_light[0] = jnp.zeros((COLORS, HS, COLS), BF16)
        edge_meta[0] = jnp.zeros((HS, 128), BF16)

    @pl.when(rows == last)
    def _():
        field[:, :, :, KR + ROWS_DEV :, :] = jnp.zeros((2, COLORS, 2, KR, COLS), BF16)
        broad[:, :, 2 * KR + ROWS_DEV :, :] = jnp.zeros((COLORS, 2, 2 * KR, COLS), BF16)
        edge_light[1] = jnp.zeros((COLORS, HS, COLS), BF16)
        edge_meta[1] = jnp.zeros((HS, 128), BF16)

    expand[...] = jnp.where(
        lax.shift_right_logical(iota((NH, COLS), 1), 4) == iota((NH, COLS), 0), 1.0, 0.0
    ).astype(BF16)
    load_idx.wait()
    load_cnt.wait()
    live = []
    for g in range(ROWS_DEV // HS):
        named = (idx_in[0, g : g + 1, :] == iota((NH, NH), 0)) & (iota((NH, NH), 1) < cnt_in[0:1, g : g + 1])
        spots = lax.dot_general(
            jnp.ones((HS, NH), BF16), jnp.where(named, 1.0, 0.0).astype(BF16),
            (((1,), (1,)), ((), ())), preferred_element_type=F32,
        )
        live.append(dot(spots.astype(BF16), expand[...]))
    live = jnp.concatenate(live, axis=0) * LIGHT_SCALE

    def light_copy(l, c, dest):
        return pltpu.make_async_remote_copy(
            src_ref=lights.at[l, c], dst_ref=lights.at[l, c],
            send_sem=light_send.at[LAYERS * l + dest, c], recv_sem=light_recv.at[l, c],
            device_id=(dest, rows), device_id_type=MESH,
        )

    def meta_copy(dest):
        return pltpu.make_async_remote_copy(
            src_ref=meta.at[depth], dst_ref=meta.at[depth],
            send_sem=meta_send.at[dest], recv_sem=meta_recv.at[depth],
            device_id=(jnp.minimum(dest, planes - 1), rows), device_id_type=MESH,
        )

    load_ct.wait()
    load_rt.wait()
    load_sil.wait()
    taps[...] = jnp.zeros_like(taps)
    for c in range(COLORS):
        taps[2 * c : 2 * c + 2, 0 : 2 * KC + 1] = ct_in[0, c].astype(F32)
        taps[8 + 2 * c : 10 + 2 * c, 0 : 2 * KR + 1] = rt_in[0, c].astype(F32)
    flip = jnp.where(iota((128, 128), 0) + iota((128, 128), 1) == 2 * KC + 1, 1.0, 0.0).astype(BF16)
    turned = dot(taps[0:8, :].astype(BF16), flip)
    plain = taps[8:16, :]
    shifted = pltpu.roll(plain, 64, 1)
    for c in range(COLORS):
        re, im = slice(2 * c, 2 * c + 1), slice(2 * c + 1, 2 * c + 2)
        taps[8 + 2 * c : 9 + 2 * c, :] = plain[re] - shifted[im]
        taps[9 + 2 * c : 10 + 2 * c, :] = plain[im] + shifted[re]
    taps[0:8, :] = turned
    meta[depth] = jnp.zeros((ROWS_DEV + HS, 128), BF16)
    meta[depth, 0:ROWS_DEV, 0:NH] = sil_in[0].astype(F32).astype(BF16)
    meta[depth, ROWS_DEV:, :] = taps[...].astype(BF16)
    for c in range(COLORS):
        load_light[c].wait()
    for c in range(COLORS):
        lights[depth, c] = (light_in[c] * live).astype(BF16)

    @pl.when(depth < 3)
    def _():
        greeted()

    for dest in range(LAYERS - 1, 0, -1):
        @pl.when(depth < dest)
        def _():
            meta_copy(dest).start()

    @pl.when(depth == 0)
    def _():
        for c in range(COLORS):
            light_copy(0, c, 3).start()
            light_copy(0, c, 1).start()

    @pl.when(depth == 1)
    def _():
        for c in range(COLORS):
            light_copy(1, c, 2).start()

    @pl.when(depth == 2)
    def _():
        for c in range(COLORS):
            light_copy(2, c, 3).start()

    @pl.when(rows > 0)
    def _():
        pl.semaphore_wait(ready, 1)
        for c in range(COLORS):
            halo_down(0, c).start()

    before = (depth, jnp.maximum(rows - 1, 0))
    after = (depth, jnp.minimum(rows + 1, last))

    def broad_copy(c, side, height):
        to = 2 * KR + ROWS_DEV if side == 0 else 2 * KR - height
        start = 2 * KR if side == 0 else 2 * KR + ROWS_DEV - height
        return pltpu.make_async_remote_copy(
            src_ref=broad.at[c, :, pl.ds(start, height), :], dst_ref=broad.at[c, :, pl.ds(to, height), :],
            send_sem=broad_send.at[c, side], recv_sem=broad_recv.at[c, side],
            device_id=(before, after)[side], device_id_type=MESH,
        )

    def edge_copies(side):
        start = 0 if side == 0 else ROWS_DEV - HS
        pairs = [(lights.at[2, c, pl.ds(start, HS), :], edge_light.at[1 - side, c]) for c in range(COLORS)]
        pairs.append((meta.at[2, pl.ds(start, HS), :], edge_meta.at[1 - side]))
        return [
            pltpu.make_async_remote_copy(
                src_ref=src, dst_ref=dst, send_sem=edge_send.at[side, i], recv_sem=edge_recv.at[side, i],
                device_id=(before, after)[side], device_id_type=MESH,
            )
            for i, (src, dst) in enumerate(pairs)
        ]

    def from_both(up, down):
        @pl.when(rows > 0)
        def _():
            up().wait_recv()

        @pl.when(rows < last)
        def _():
            down().wait_recv()

    def to_both(down, up):
        @pl.when(rows > 0)
        def _():
            down().start()

        @pl.when(rows < last)
        def _():
            up().start()

    def sent_both(down, up):
        @pl.when(rows > 0)
        def _():
            down().wait_send()

        @pl.when(rows < last)
        def _():
            up().wait_send()

    def wait_meta(l):
        @pl.when(depth > l)
        def _():
            pltpu.make_async_remote_copy(
                src_ref=meta.at[l], dst_ref=meta.at[l], send_sem=meta_send.at[0], recv_sem=meta_recv.at[l],
                device_id=(depth, rows), device_id_type=MESH,
            ).wait_recv()

    def wait_light(l, c):
        @pl.when(depth > l)
        def _():
            light_copy(l, c, 3).wait_recv()

    def opening(edges, height):
        within = (iota((height, COLS), 1) & (HS - 1)).astype(F32)
        return jnp.where(within < dot(edges, expand[...]), 1.0, 0.0)

    def narrow_rows(l, slot):
        for c in range(COLORS):
            for comp in range(2):
                line = meta[l, ROWS_DEV:, :].astype(F32)[8 + 2 * c + comp : 9 + 2 * c + comp]
                row_mat[slot, c, ROWS_DEV * comp : ROWS_DEV * (comp + 1), :] = pltpu.roll(
                    jnp.broadcast_to(line, (ROWS_DEV, 128)), 0, 1, stride=1, stride_axis=0
                ).astype(BF16)
        clear[slot] = opening(meta[l, 0:ROWS_DEV, 0:NH], ROWS_DEV)

    def wide_rows(l):
        for c in range(COLORS):
            for comp in range(2):
                line = meta[l, ROWS_DEV:, :].astype(F32)[8 + 2 * c + comp : 9 + 2 * c + comp]
                first = iota((1, 128), 1) < 64
                none = jnp.zeros((1, 128), F32)
                line = jnp.concatenate([jnp.where(first, line, 0.0), none], axis=1) + pltpu.roll(
                    jnp.concatenate([jnp.where(first, 0.0, line), none], axis=1), 32, 1
                )
                row_wide[c, EXT * comp : EXT * (comp + 1), :] = pltpu.roll(
                    jnp.broadcast_to(line, (EXT, 256)), 0, 1, stride=1, stride_axis=0
                )[:, 0 : 2 * (EXT + ROWS_DEV)].astype(BF16)

    def columns(l, slot):
        lines = meta[l, ROWS_DEV:, :].astype(F32)
        below = iota((128, 128), 0) > iota((128, 128), 1)
        above = iota((128, 128), 0) < iota((128, 128), 1)
        for c in range(COLORS):
            turn = [
                pltpu.roll(
                    jnp.broadcast_to(lines[2 * c + comp : 2 * c + comp + 1], (128, 128)),
                    0, 1, stride=1, stride_axis=0,
                )
                for comp in range(2)
            ]
            for half, inside in enumerate((below, above)):
                real = jnp.where(inside, turn[0], 0.0)
                imag = jnp.where(inside, turn[1], 0.0)
                top, low = 128 * half, 256 + 128 * half
                col_mat[slot, c, top : top + 128, 0:128] = real.astype(BF16)
                col_mat[slot, c, top : top + 128, 128:256] = imag.astype(BF16)
                col_mat[slot, c, low : low + 128, 0:128] = (-imag).astype(BF16)
                col_mat[slot, c, low : low + 128, 128:256] = real.astype(BF16)

    def transform(c, value, spot):
        half_done = dot(left_in[...], value).astype(BF16)
        for t in range(TILES):
            here = slice(128 * t, 128 * (t + 1))
            mixed[spot, c, ROWS_DEV * t : ROWS_DEV * (t + 1), 0:128] = half_done[0:ROWS_DEV, here]
            mixed[spot, c, ROWS_DEV * t : ROWS_DEV * (t + 1), 128:256] = half_done[ROWS_DEV:, here]
        return dot(mixed[spot, c], right_in[...])

    def keep_transform(c, value, spot, ref, start):
        done = transform(c, value, spot)
        for t in range(TILES):
            for comp in range(2):
                ref[c, comp, start : start + ROWS_DEV, 128 * t : 128 * (t + 1)] = done[
                    ROWS_DEV * t : ROWS_DEV * (t + 1), 128 * comp : 128 * (comp + 1)
                ]

    def propagate(value, mat, pad, slot, c, height):
        rowed = dot(mat[c], value)
        wide = jnp.concatenate([rowed, jnp.zeros((2 * height, 128), F32)], axis=1)
        pad[c] = pltpu.roll(wide, 64, 1).astype(BF16)
        windows = jnp.concatenate(
            [
                jnp.concatenate(
                    [pad[c, 0:height, 128 * t : 128 * t + 256], pad[c, height:, 128 * t : 128 * t + 256]], axis=1
                )
                for t in range(TILES)
            ],
            axis=0,
        )
        return dot(windows, col_mat[slot, c])

    def pieces():
        for t in range(TILES):
            for comp in range(2):
                yield t, comp, slice(128 * t, 128 * (t + 1)), slice(128 * comp, 128 * (comp + 1))

    def step(l, c, value, store):
        done = transform(c, lights[l, c], 0)
        columned = propagate(value, row_mat.at[0], vpad, 0, c, ROWS_DEV)
        for t, comp, here, side in pieces():
            band = slice(ROWS_DEV * t, ROWS_DEV * (t + 1))
            store(comp, here, (columned[band, side] * clear[0, :, here] + done[band, side]).astype(BF16))

    def step_on_kept(c, value, store, slot, col_slot):
        columned = propagate(value, row_mat.at[slot], vpad, col_slot, c, ROWS_DEV)
        for t, comp, here, side in pieces():
            band = slice(ROWS_DEV * t, ROWS_DEV * (t + 1))
            value = columned[band, side] * clear[slot, :, here] + stereo[c, comp, :, here]
            store(comp, here, value.astype(BF16))

    @pl.when(depth == 1)
    def _():
        for c in range(COLORS):
            light_copy(0, c, 2).wait_recv()
            light_copy(0, c, 2).start()

    @pl.when(depth == 2)
    def _():
        for c in range(COLORS):
            light_copy(1, c, 3).wait_recv()
            light_copy(1, c, 3).start()

    wait_meta(0)
    narrow_rows(0, 0)
    columns(0, 0)

    for c in range(COLORS):
        load_inc[c].wait()
    load_left.wait()
    load_right.wait()
    eager = lax.rem(rows, 16) == 0

    @pl.when(eager)
    def _():
        for c in range(COLORS):
            @pl.when(depth > 1)
            def _():
                wait_light(0, c)

            keep_transform(c, lights[0, c], 0, stereo, 0)

    for c in range(COLORS):
        @pl.when((depth > 1) & (lax.rem(rows, 16) > 0))
        def _():
            wait_light(0, c)

        from_both(lambda: halo_up(0, c), lambda: halo_down(0, c))

        def store(comp, here, value):
            field[1, c, comp, KR : KR + ROWS_DEV, here] = value
            out[0, c, comp, :, here] = value

        @pl.when(eager)
        def _():
            step_on_kept(c, field[0, c].reshape(2 * EXT, COLS), store, 0, 0)

        @pl.when(lax.rem(rows, 16) > 0)
        def _():
            step(0, c, field[0, c].reshape(2 * EXT, COLS), store)

        @pl.when(depth > 0)
        def _():
            to_both(lambda: halo_down(1, c), lambda: halo_up(1, c))

    @pl.when(depth == 3)
    def _():
        wait_meta(2)
        for c in range(COLORS):
            wait_light(2, c)

        @pl.when(rows > 0)
        def _():
            for copy in edge_copies(0):
                copy.start()

        @pl.when(rows < last)
        def _():
            for copy in edge_copies(1):
                copy.start()

    def prepare_last():
        @pl.when(depth == 2)
        def _():
            narrow_rows(2, 1)
            columns(2, 1)
            for c in range(COLORS):
                keep_transform(c, lights[2, c], 0, stereo, 0)

        @pl.when(depth == 3)
        def _():
            narrow_rows(3, 1)
            wide_rows(2)
            columns(3, 2)
            columns(2, 1)
            for c in range(COLORS):
                keep_transform(c, lights[3, c], 0, stereo, 0)

    @pl.when(eager)
    def _():
        prepare_last()

    @pl.when(depth > 0)
    def _():
        wait_meta(1)
        narrow_rows(1, 0)
        columns(1, 0)
        for c in range(COLORS):
            @pl.when((depth == 3))
            def _():
                wait_light(1, c)

            from_both(lambda: halo_up(1, c), lambda: halo_down(1, c))

            def store(comp, here, value):
                broad[c, comp, 2 * KR : 2 * KR + ROWS_DEV, here] = value
                out[0, c, comp, :, here] = value

            step(1, c, field[1, c].reshape(2 * EXT, COLS), store)

            @pl.when(depth == 2)
            def _():
                to_both(lambda: broad_copy(c, 0, KR), lambda: broad_copy(c, 1, KR))

            @pl.when(depth == 3)
            def _():
                to_both(lambda: broad_copy(c, 0, 2 * KR), lambda: broad_copy(c, 1, 2 * KR))

    @pl.when(lax.rem(rows, 16) > 0)
    def _():
        prepare_last()

    @pl.when(depth == 2)
    def _():
        for c in range(COLORS):
            from_both(lambda: broad_copy(c, 1, KR), lambda: broad_copy(c, 0, KR))

            def store(comp, here, value):
                out[0, c, comp, :, here] = value

            step_on_kept(c, broad[c, :, KR : KR + EXT, :].reshape(2 * EXT, COLS), store, 1, 1)

    @pl.when(depth == 3)
    def _():
        @pl.when(rows > 0)
        def _():
            for copy in edge_copies(1):
                copy.wait_recv()

        @pl.when(rows < last)
        def _():
            for copy in edge_copies(0):
                copy.wait_recv()

        clear_wide[...] = opening(
            jnp.concatenate([edge_meta[0], meta[2, 0:ROWS_DEV, :], edge_meta[1]], axis=0)[:, 0:NH], EXT
        )
        for c in range(COLORS):
            upper = jnp.concatenate([edge_light[0, c], lights[2, c, 0:HS, :]], axis=0)
            lower = jnp.concatenate([lights[2, c, HS:, :], edge_light[1, c]], axis=0)
            keep_transform(c, upper, 0, stereo_wide, 0)
            keep_transform(c, lower, 1, stereo_wide, ROWS_DEV)

        def finish(c):
            def store(comp, here, value):
                out[0, c, comp, :, here] = value

            step_on_kept(c, inner[c].reshape(2 * EXT, COLS), store, 1, 2)

        for c in range(COLORS):
            from_both(lambda: broad_copy(c, 1, 2 * KR), lambda: broad_copy(c, 0, 2 * KR))
            columned = propagate(
                broad[c].reshape(2 * (EXT + ROWS_DEV), COLS), row_wide, vpad_wide, 1, c, EXT
            )
            for t, comp, here, side in pieces():
                band = slice(EXT * t, EXT * (t + 1))
                value = columned[band, side] * clear_wide[:, here] + stereo_wide[c, comp, :, here]
                inner[c, comp, :, here] = value.astype(BF16)
            if c > 0:
                finish(c - 1)
        finish(COLORS - 1)

    for c in range(COLORS):
        sent_both(lambda: halo_down(0, c), lambda: halo_up(0, c))

        @pl.when(depth > 0)
        def _():
            sent_both(lambda: halo_down(1, c), lambda: halo_up(1, c))

        @pl.when(depth == 2)
        def _():
            sent_both(lambda: broad_copy(c, 0, KR), lambda: broad_copy(c, 1, KR))

        @pl.when(depth == 3)
        def _():
            sent_both(lambda: broad_copy(c, 0, 2 * KR), lambda: broad_copy(c, 1, 2 * KR))

    @pl.when((depth == 3) & (rows > 0))
    def _():
        for copy in edge_copies(0):
            copy.wait_send()

    @pl.when((depth == 3) & (rows < last))
    def _():
        for copy in edge_copies(1):
            copy.wait_send()

    for dest in range(1, LAYERS):
        @pl.when(depth < dest)
        def _():
            meta_copy(dest).wait_send()

    for at, l, dest in ((0, 0, 3), (0, 0, 1), (1, 1, 2), (2, 2, 3), (2, 1, 3), (1, 0, 2)):
        @pl.when(depth == at)
        def _():
            for c in range(COLORS):
                light_copy(l, c, dest).wait_send()


def body(incident, row_taps, col_taps, hogel_light, silhouette, fill_counts, hogel_index):
    left, right = dft_constants()
    anywhere = pl.BlockSpec(memory_space=pltpu.HBM)
    dma = pltpu.SemaphoreType.DMA
    return pl.pallas_call(
        kernel,
        name="hologram",
        out_shape=jax.ShapeDtypeStruct((1,) + incident.shape, BF16),
        in_specs=[anywhere] * 9,
        out_specs=pl.BlockSpec(memory_space=pltpu.VMEM),
        scratch_shapes=[
            pltpu.VMEM((2, COLORS, 2, EXT, COLS), BF16),
            pltpu.VMEM((COLORS, 2, EXT + ROWS_DEV, COLS), BF16),
            pltpu.VMEM((COLORS, 2, EXT, COLS), BF16),
            pltpu.VMEM((LAYERS, COLORS, ROWS_DEV, COLS), BF16),
            pltpu.VMEM((2, COLORS, HS, COLS), BF16),
            pltpu.VMEM((LAYERS, ROWS_DEV + HS, 128), BF16),
            pltpu.VMEM((2, HS, 128), BF16),
            pltpu.VMEM((COLORS, ROWS_DEV, COLS), F32),
            pltpu.VMEM(row_taps.shape, BF16),
            pltpu.VMEM(col_taps.shape, BF16),
            pltpu.VMEM(silhouette.shape, jnp.int32),
            pltpu.VMEM(fill_counts.shape, jnp.int32),
            pltpu.VMEM(hogel_index.shape, jnp.int32),
            pltpu.VMEM(left.shape, BF16),
            pltpu.VMEM(right.shape, BF16),
            pltpu.VMEM((16, 128), F32),
            pltpu.VMEM((NH, COLS), BF16),
            pltpu.VMEM((2, COLORS, 2 * ROWS_DEV, 128), BF16),
            pltpu.VMEM((COLORS, 2 * EXT, 2 * (EXT + ROWS_DEV)), BF16),
            pltpu.VMEM((3, COLORS, 512, 256), BF16),
            pltpu.VMEM((2, ROWS_DEV, COLS), F32),
            pltpu.VMEM((EXT, COLS), F32),
            pltpu.VMEM((COLORS, 2, ROWS_DEV, COLS), F32),
            pltpu.VMEM((COLORS, 2, EXT, COLS), F32),
            pltpu.VMEM((COLORS, 2 * ROWS_DEV, COLS + 128), BF16),
            pltpu.VMEM((COLORS, 2 * EXT, COLS + 128), BF16),
            pltpu.VMEM((2, COLORS, ROWS_DEV * TILES, 256), BF16),
            dma((13,)),
            dma((2, COLORS, 2)),
            dma((2, COLORS, 2)),
            dma((COLORS, 2)),
            dma((COLORS, 2)),
            dma((2, COLORS + 1)),
            dma((2, COLORS + 1)),
            dma((LAYERS * LAYERS, COLORS)),
            dma((LAYERS, COLORS)),
            dma((LAYERS,)),
            dma((LAYERS,)),
            pltpu.SemaphoreType.REGULAR,
        ],
        compiler_params=pltpu.CompilerParams(
            collective_id=0, has_side_effects=True, vmem_limit_bytes=40 << 20
        ),
    )(*[
        pltpu.with_memory_space_constraint(x, pltpu.HBM)
        for x in (
            incident, row_taps, col_taps, hogel_light, silhouette, fill_counts, hogel_index,
            jnp.asarray(left), jnp.asarray(right),
        )
    ])


def solution(mesh):
    placed = (
        P(None, None, "rows", None),
        P("depth", None, None, None),
        P("depth", None, None, None),
        P("depth", None, "rows", None),
        P("depth", "rows", None),
        P("depth", "rows"),
        P("depth", "rows", None),
    )
    return jax.shard_map(
        body,
        mesh=mesh,
        in_specs=placed,
        out_specs=P("depth", None, None, "rows", None),
        check_vma=False,
    )
```

```python
import math

import jax
import jax.numpy as jnp
import ml_dtypes
import numpy as np
from jax import lax
from jax.experimental import pallas as pl
from jax.experimental.pallas import tpu as pltpu
from jax.sharding import PartitionSpec as P

HS = 16
KR = 16
KC = 63
COLORS = 3
ROWS_DEV = 32
COLS = 1024
LAYERS = 4
NH = 64
TILES = COLS // 128
EXT = ROWS_DEV + 2 * KR
TABLE_SCALE = 1.132805
LIGHT_SCALE = 1.0 / (HS * TABLE_SCALE * TABLE_SCALE)
MESH = pl.DeviceIdType.MESH
F32 = jnp.float32
BF16 = jnp.bfloat16


def dft_constants():
    counter = np.arange(HS)
    angles = (counter[:, None] * counter[None, :] % HS) * (2.0 * math.pi / HS)
    cos_tab, sin_tab = TABLE_SCALE * np.cos(angles), TABLE_SCALE * np.sin(angles)
    groups, per_block = ROWS_DEV // HS, 128 // HS
    left = np.concatenate([np.kron(np.eye(groups), cos_tab), np.kron(np.eye(groups), -sin_tab)], axis=0)
    cos_big, sin_big = np.kron(np.eye(per_block), cos_tab), np.kron(np.eye(per_block), sin_tab)
    right = np.block([[cos_big, -sin_big], [sin_big, cos_big]])
    return left.astype(ml_dtypes.bfloat16), right.astype(ml_dtypes.bfloat16)


def dot(a, b):
    return jnp.dot(a, b, preferred_element_type=F32)


def iota(shape, dim):
    return lax.broadcasted_iota(jnp.int32, shape, dim)


def kernel(
    inc, row_taps, col_taps, light, sil, counts, index, left, right, out,
    field, broad, inner, lights, edge_light, meta, edge_meta,
    light_in, rt_in, ct_in, sil_in, cnt_in, idx_in, left_in, right_in,
    taps, expand, row_mat, row_wide, col_mat, clear, clear_wide, stereo, stereo_wide, vpad, vpad_wide, mixed,
    load_sem, halo_send, halo_recv, broad_send, broad_recv, edge_send, edge_recv,
    light_send, light_recv, meta_send, meta_recv, ready,
):
    depth, rows = lax.axis_index("depth"), lax.axis_index("rows")
    last = lax.axis_size("rows") - 1
    planes = lax.axis_size("depth")

    barrier = pltpu.get_barrier_semaphore()

    @pl.when(rows > 0)
    def _():
        pl.semaphore_signal(barrier, inc=1, device_id=(depth, rows - 1), device_id_type=MESH)

    for back in range(1, LAYERS):
        @pl.when(depth >= back)
        def _():
            pl.semaphore_signal(barrier, inc=1, device_id=(depth - back, rows), device_id_type=MESH)

    def halo_down(l, c):
        return pltpu.make_async_remote_copy(
            src_ref=field.at[l, c, :, pl.ds(KR, KR), :] if l else inc.at[c, :, pl.ds(0, KR), :],
            dst_ref=field.at[l, c, :, pl.ds(KR + ROWS_DEV, KR), :],
            send_sem=halo_send.at[l, c, 0], recv_sem=halo_recv.at[l, c, 0],
            device_id=(depth, jnp.maximum(rows - 1, 0)), device_id_type=MESH,
        )

    def halo_up(l, c):
        return pltpu.make_async_remote_copy(
            src_ref=field.at[l, c, :, pl.ds(ROWS_DEV, KR), :] if l else inc.at[c, :, pl.ds(KR, KR), :],
            dst_ref=field.at[l, c, :, pl.ds(0, KR), :],
            send_sem=halo_send.at[l, c, 1], recv_sem=halo_recv.at[l, c, 1],
            device_id=(depth, jnp.minimum(rows + 1, last)), device_id_type=MESH,
        )

    greetings = planes - 1 - depth + jnp.where(rows < last, 1, 0)

    def greeted():
        @pl.when(greetings > 0)
        def _():
            pl.semaphore_wait(barrier, greetings)

        @pl.when(rows < last)
        def _():
            pl.semaphore_signal(ready, inc=1, device_id=(depth, rows + 1), device_id_type=MESH)
            for c in range(COLORS):
                halo_up(0, c).start()

    @pl.when(depth == 3)
    def _():
        greeted()

    loads = []
    pairs = [(inc.at[c], field.at[0, c, :, pl.ds(KR, ROWS_DEV), :]) for c in range(COLORS)]
    pairs += [(light.at[0, c], light_in.at[c]) for c in range(COLORS)]
    pairs += [(index, idx_in), (counts, cnt_in), (col_taps, ct_in), (row_taps, rt_in), (sil, sil_in)]
    pairs += [(left, left_in), (right, right_in)]
    for i, (src, dst) in enumerate(pairs):
        copy = pltpu.make_async_copy(src, dst, load_sem.at[i])
        copy.start()
        loads.append(copy)
    load_inc, load_light = loads[:COLORS], loads[COLORS : 2 * COLORS]
    load_idx, load_cnt, load_ct, load_rt, load_sil, load_left, load_right = loads[2 * COLORS :]

    @pl.when(rows == 0)
    def _():
        field[:, :, :, 0:KR, :] = jnp.zeros((2, COLORS, 2, KR, COLS), BF16)
        broad[:, :, 0 : 2 * KR, :] = jnp.zeros((COLORS, 2, 2 * KR, COLS), BF16)
        edge_light[0] = jnp.zeros((COLORS, HS, COLS), BF16)
        edge_meta[0] = jnp.zeros((HS, 128), BF16)

    @pl.when(rows == last)
    def _():
        field[:, :, :, KR + ROWS_DEV :, :] = jnp.zeros((2, COLORS, 2, KR, COLS), BF16)
        broad[:, :, 2 * KR + ROWS_DEV :, :] = jnp.zeros((COLORS, 2, 2 * KR, COLS), BF16)
        edge_light[1] = jnp.zeros((COLORS, HS, COLS), BF16)
        edge_meta[1] = jnp.zeros((HS, 128), BF16)

    expand[...] = jnp.where(
        lax.shift_right_logical(iota((NH, COLS), 1), 4) == iota((NH, COLS), 0), 1.0, 0.0
    ).astype(BF16)
    load_idx.wait()
    load_cnt.wait()
    live = []
    for g in range(ROWS_DEV // HS):
        named = (idx_in[0, g : g + 1, :] == iota((NH, NH), 0)) & (iota((NH, NH), 1) < cnt_in[0:1, g : g + 1])
        spots = lax.dot_general(
            jnp.ones((HS, NH), BF16), jnp.where(named, 1.0, 0.0).astype(BF16),
            (((1,), (1,)), ((), ())), preferred_element_type=F32,
        )
        live.append(dot(spots.astype(BF16), expand[...]))
    live = jnp.concatenate(live, axis=0) * LIGHT_SCALE

    def light_copy(l, c, dest):
        return pltpu.make_async_remote_copy(
            src_ref=lights.at[l, c], dst_ref=lights.at[l, c],
            send_sem=light_send.at[LAYERS * l + dest, c], recv_sem=light_recv.at[l, c],
            device_id=(dest, rows), device_id_type=MESH,
        )

    def meta_copy(dest):
        return pltpu.make_async_remote_copy(
            src_ref=meta.at[depth], dst_ref=meta.at[depth],
            send_sem=meta_send.at[dest], recv_sem=meta_recv.at[depth],
            device_id=(jnp.minimum(dest, planes - 1), rows), device_id_type=MESH,
        )

    load_ct.wait()
    load_rt.wait()
    load_sil.wait()
    taps[...] = jnp.zeros_like(taps)
    for c in range(COLORS):
        taps[2 * c : 2 * c + 2, 0 : 2 * KC + 1] = ct_in[0, c].astype(F32)
        taps[8 + 2 * c : 10 + 2 * c, 0 : 2 * KR + 1] = rt_in[0, c].astype(F32)
    flip = jnp.where(iota((128, 128), 0) + iota((128, 128), 1) == 2 * KC + 1, 1.0, 0.0).astype(BF16)
    turned = dot(taps[0:8, :].astype(BF16), flip)
    plain = taps[8:16, :]
    shifted = pltpu.roll(plain, 64, 1)
    for c in range(COLORS):
        re, im = slice(2 * c, 2 * c + 1), slice(2 * c + 1, 2 * c + 2)
        taps[8 + 2 * c : 9 + 2 * c, :] = plain[re] - shifted[im]
        taps[9 + 2 * c : 10 + 2 * c, :] = plain[im] + shifted[re]
    taps[0:8, :] = turned
    meta[depth] = jnp.zeros((ROWS_DEV + HS, 128), BF16)
    meta[depth, 0:ROWS_DEV, 0:NH] = sil_in[0].astype(F32).astype(BF16)
    meta[depth, ROWS_DEV:, :] = taps[...].astype(BF16)
    for c in range(COLORS):
        load_light[c].wait()
    for c in range(COLORS):
        lights[depth, c] = (light_in[c] * live).astype(BF16)

    @pl.when(depth < 3)
    def _():
        greeted()

    for dest in range(LAYERS - 1, 0, -1):
        @pl.when(depth < dest)
        def _():
            meta_copy(dest).start()

    @pl.when(depth == 0)
    def _():
        for c in range(COLORS):
            light_copy(0, c, 3).start()
            light_copy(0, c, 1).start()

    @pl.when(depth == 1)
    def _():
        for c in range(COLORS):
            light_copy(1, c, 2).start()

    @pl.when(depth == 2)
    def _():
        for c in range(COLORS):
            light_copy(2, c, 3).start()

    @pl.when(rows > 0)
    def _():
        pl.semaphore_wait(ready, 1)
        for c in range(COLORS):
            halo_down(0, c).start()

    before = (depth, jnp.maximum(rows - 1, 0))
    after = (depth, jnp.minimum(rows + 1, last))

    def broad_copy(c, side, height):
        to = 2 * KR + ROWS_DEV if side == 0 else 2 * KR - height
        start = 2 * KR if side == 0 else 2 * KR + ROWS_DEV - height
        return pltpu.make_async_remote_copy(
            src_ref=broad.at[c, :, pl.ds(start, height), :], dst_ref=broad.at[c, :, pl.ds(to, height), :],
            send_sem=broad_send.at[c, side], recv_sem=broad_recv.at[c, side],
            device_id=(before, after)[side], device_id_type=MESH,
        )

    def edge_copies(side):
        start = 0 if side == 0 else ROWS_DEV - HS
        pairs = [(lights.at[2, c, pl.ds(start, HS), :], edge_light.at[1 - side, c]) for c in range(COLORS)]
        pairs.append((meta.at[2, pl.ds(start, HS), :], edge_meta.at[1 - side]))
        return [
            pltpu.make_async_remote_copy(
                src_ref=src, dst_ref=dst, send_sem=edge_send.at[side, i], recv_sem=edge_recv.at[side, i],
                device_id=(before, after)[side], device_id_type=MESH,
            )
            for i, (src, dst) in enumerate(pairs)
        ]

    def from_both(up, down):
        @pl.when(rows > 0)
        def _():
            up().wait_recv()

        @pl.when(rows < last)
        def _():
            down().wait_recv()

    def to_both(down, up):
        @pl.when(rows > 0)
        def _():
            down().start()

        @pl.when(rows < last)
        def _():
            up().start()

    def sent_both(down, up):
        @pl.when(rows > 0)
        def _():
            down().wait_send()

        @pl.when(rows < last)
        def _():
            up().wait_send()

    def wait_meta(l):
        @pl.when(depth > l)
        def _():
            pltpu.make_async_remote_copy(
                src_ref=meta.at[l], dst_ref=meta.at[l], send_sem=meta_send.at[0], recv_sem=meta_recv.at[l],
                device_id=(depth, rows), device_id_type=MESH,
            ).wait_recv()

    def wait_light(l, c):
        @pl.when(depth > l)
        def _():
            light_copy(l, c, 3).wait_recv()

    def opening(edges, height):
        within = (iota((height, COLS), 1) & (HS - 1)).astype(F32)
        return jnp.where(within < dot(edges, expand[...]), 1.0, 0.0)

    def narrow_rows(l, slot):
        for c in range(COLORS):
            for comp in range(2):
                line = meta[l, ROWS_DEV:, :].astype(F32)[8 + 2 * c + comp : 9 + 2 * c + comp]
                row_mat[slot, c, ROWS_DEV * comp : ROWS_DEV * (comp + 1), :] = pltpu.roll(
                    jnp.broadcast_to(line, (ROWS_DEV, 128)), 0, 1, stride=1, stride_axis=0
                ).astype(BF16)
        clear[slot] = opening(meta[l, 0:ROWS_DEV, 0:NH], ROWS_DEV)

    def wide_rows(l):
        for c in range(COLORS):
            for comp in range(2):
                line = meta[l, ROWS_DEV:, :].astype(F32)[8 + 2 * c + comp : 9 + 2 * c + comp]
                first = iota((1, 128), 1) < 64
                none = jnp.zeros((1, 128), F32)
                line = jnp.concatenate([jnp.where(first, line, 0.0), none], axis=1) + pltpu.roll(
                    jnp.concatenate([jnp.where(first, 0.0, line), none], axis=1), 32, 1
                )
                row_wide[c, EXT * comp : EXT * (comp + 1), :] = pltpu.roll(
                    jnp.broadcast_to(line, (EXT, 256)), 0, 1, stride=1, stride_axis=0
                )[:, 0 : 2 * (EXT + ROWS_DEV)].astype(BF16)

    def columns(l, slot):
        lines = meta[l, ROWS_DEV:, :].astype(F32)
        below = iota((128, 128), 0) > iota((128, 128), 1)
        above = iota((128, 128), 0) < iota((128, 128), 1)
        for c in range(COLORS):
            turn = [
                pltpu.roll(
                    jnp.broadcast_to(lines[2 * c + comp : 2 * c + comp + 1], (128, 128)),
                    0, 1, stride=1, stride_axis=0,
                )
                for comp in range(2)
            ]
            for half, inside in enumerate((below, above)):
                real = jnp.where(inside, turn[0], 0.0)
                imag = jnp.where(inside, turn[1], 0.0)
                top, low = 128 * half, 256 + 128 * half
                col_mat[slot, c, top : top + 128, 0:128] = real.astype(BF16)
                col_mat[slot, c, top : top + 128, 128:256] = imag.astype(BF16)
                col_mat[slot, c, low : low + 128, 0:128] = (-imag).astype(BF16)
                col_mat[slot, c, low : low + 128, 128:256] = real.astype(BF16)

    def transform(c, value, spot):
        half_done = dot(left_in[...], value).astype(BF16)
        for t in range(TILES):
            here = slice(128 * t, 128 * (t + 1))
            mixed[spot, c, ROWS_DEV * t : ROWS_DEV * (t + 1), 0:128] = half_done[0:ROWS_DEV, here]
            mixed[spot, c, ROWS_DEV * t : ROWS_DEV * (t + 1), 128:256] = half_done[ROWS_DEV:, here]
        return dot(mixed[spot, c], right_in[...])

    def keep_transform(c, value, spot, ref, start):
        done = transform(c, value, spot)
        for t in range(TILES):
            for comp in range(2):
                ref[c, comp, start : start + ROWS_DEV, 128 * t : 128 * (t + 1)] = done[
                    ROWS_DEV * t : ROWS_DEV * (t + 1), 128 * comp : 128 * (comp + 1)
                ]

    def propagate(value, mat, pad, slot, c, height):
        rowed = dot(mat[c], value)
        wide = jnp.concatenate([rowed, jnp.zeros((2 * height, 128), F32)], axis=1)
        pad[c] = pltpu.roll(wide, 64, 1).astype(BF16)
        windows = jnp.concatenate(
            [
                jnp.concatenate(
                    [pad[c, 0:height, 128 * t : 128 * t + 256], pad[c, height:, 128 * t : 128 * t + 256]], axis=1
                )
                for t in range(TILES)
            ],
            axis=0,
        )
        return dot(windows, col_mat[slot, c])

    def pieces():
        for t in range(TILES):
            for comp in range(2):
                yield t, comp, slice(128 * t, 128 * (t + 1)), slice(128 * comp, 128 * (comp + 1))

    def step(l, c, value, store):
        done = transform(c, lights[l, c], 0)
        columned = propagate(value, row_mat.at[0], vpad, 0, c, ROWS_DEV)
        for t, comp, here, side in pieces():
            band = slice(ROWS_DEV * t, ROWS_DEV * (t + 1))
            store(comp, here, (columned[band, side] * clear[0, :, here] + done[band, side]).astype(BF16))

    def step_on_kept(c, value, store, slot, col_slot):
        columned = propagate(value, row_mat.at[slot], vpad, col_slot, c, ROWS_DEV)
        for t, comp, here, side in pieces():
            band = slice(ROWS_DEV * t, ROWS_DEV * (t + 1))
            value = columned[band, side] * clear[slot, :, here] + stereo[c, comp, :, here]
            store(comp, here, value.astype(BF16))

    @pl.when(depth == 1)
    def _():
        for c in range(COLORS):
            light_copy(0, c, 2).wait_recv()
            light_copy(0, c, 2).start()

    wait_meta(0)
    narrow_rows(0, 0)
    columns(0, 0)

    @pl.when(depth == 2)
    def _():
        for c in range(COLORS):
            light_copy(1, c, 3).wait_recv()
            light_copy(1, c, 3).start()

    for c in range(COLORS):
        load_inc[c].wait()
    load_left.wait()
    load_right.wait()
    eager = lax.rem(rows, 16) == 0

    @pl.when(eager)
    def _():
        for c in range(COLORS):
            @pl.when(depth > 1)
            def _():
                wait_light(0, c)

            keep_transform(c, lights[0, c], 0, stereo, 0)

    for c in range(COLORS):
        @pl.when((depth > 1) & (lax.rem(rows, 16) > 0))
        def _():
            wait_light(0, c)

        from_both(lambda: halo_up(0, c), lambda: halo_down(0, c))

        def store(comp, here, value):
            field[1, c, comp, KR : KR + ROWS_DEV, here] = value
            out[0, c, comp, :, here] = value

        @pl.when(eager)
        def _():
            step_on_kept(c, field[0, c].reshape(2 * EXT, COLS), store, 0, 0)

        @pl.when(lax.rem(rows, 16) > 0)
        def _():
            step(0, c, field[0, c].reshape(2 * EXT, COLS), store)

        @pl.when(depth > 0)
        def _():
            to_both(lambda: halo_down(1, c), lambda: halo_up(1, c))

    @pl.when(depth == 3)
    def _():
        wait_meta(2)
        for c in range(COLORS):
            wait_light(2, c)

        @pl.when(rows > 0)
        def _():
            for copy in edge_copies(0):
                copy.start()

        @pl.when(rows < last)
        def _():
            for copy in edge_copies(1):
                copy.start()

    def prepare_last():
        @pl.when(depth == 2)
        def _():
            narrow_rows(2, 1)
            columns(2, 1)
            for c in range(COLORS):
                keep_transform(c, lights[2, c], 0, stereo, 0)

        @pl.when(depth == 3)
        def _():
            narrow_rows(3, 1)
            wide_rows(2)
            columns(3, 2)
            columns(2, 1)
            for c in range(COLORS):
                keep_transform(c, lights[3, c], 0, stereo, 0)

    @pl.when(eager)
    def _():
        prepare_last()

    @pl.when(depth > 0)
    def _():
        wait_meta(1)
        narrow_rows(1, 0)
        columns(1, 0)
        for c in range(COLORS):
            @pl.when((depth == 3))
            def _():
                wait_light(1, c)

            from_both(lambda: halo_up(1, c), lambda: halo_down(1, c))

            def store(comp, here, value):
                broad[c, comp, 2 * KR : 2 * KR + ROWS_DEV, here] = value
                out[0, c, comp, :, here] = value

            step(1, c, field[1, c].reshape(2 * EXT, COLS), store)

            @pl.when(depth == 2)
            def _():
                to_both(lambda: broad_copy(c, 0, KR), lambda: broad_copy(c, 1, KR))

            @pl.when(depth == 3)
            def _():
                to_both(lambda: broad_copy(c, 0, 2 * KR), lambda: broad_copy(c, 1, 2 * KR))

    @pl.when(lax.rem(rows, 16) > 0)
    def _():
        prepare_last()

    @pl.when(depth == 2)
    def _():
        for c in range(COLORS):
            from_both(lambda: broad_copy(c, 1, KR), lambda: broad_copy(c, 0, KR))

            def store(comp, here, value):
                out[0, c, comp, :, here] = value

            step_on_kept(c, broad[c, :, KR : KR + EXT, :].reshape(2 * EXT, COLS), store, 1, 1)

    @pl.when(depth == 3)
    def _():
        @pl.when(rows > 0)
        def _():
            for copy in edge_copies(1):
                copy.wait_recv()

        @pl.when(rows < last)
        def _():
            for copy in edge_copies(0):
                copy.wait_recv()

        clear_wide[...] = opening(
            jnp.concatenate([edge_meta[0], meta[2, 0:ROWS_DEV, :], edge_meta[1]], axis=0)[:, 0:NH], EXT
        )
        for c in range(COLORS):
            upper = jnp.concatenate([edge_light[0, c], lights[2, c, 0:HS, :]], axis=0)
            lower = jnp.concatenate([lights[2, c, HS:, :], edge_light[1, c]], axis=0)
            keep_transform(c, upper, 0, stereo_wide, 0)
            keep_transform(c, lower, 1, stereo_wide, ROWS_DEV)

        def finish(c):
            def store(comp, here, value):
                out[0, c, comp, :, here] = value

            step_on_kept(c, inner[c].reshape(2 * EXT, COLS), store, 1, 2)

        for c in range(COLORS):
            from_both(lambda: broad_copy(c, 1, 2 * KR), lambda: broad_copy(c, 0, 2 * KR))
            columned = propagate(
                broad[c].reshape(2 * (EXT + ROWS_DEV), COLS), row_wide, vpad_wide, 1, c, EXT
            )
            for t, comp, here, side in pieces():
                band = slice(EXT * t, EXT * (t + 1))
                value = columned[band, side] * clear_wide[:, here] + stereo_wide[c, comp, :, here]
                inner[c, comp, :, here] = value.astype(BF16)
            if c > 0:
                finish(c - 1)
        finish(COLORS - 1)

    for c in range(COLORS):
        sent_both(lambda: halo_down(0, c), lambda: halo_up(0, c))

        @pl.when(depth > 0)
        def _():
            sent_both(lambda: halo_down(1, c), lambda: halo_up(1, c))

        @pl.when(depth == 2)
        def _():
            sent_both(lambda: broad_copy(c, 0, KR), lambda: broad_copy(c, 1, KR))

        @pl.when(depth == 3)
        def _():
            sent_both(lambda: broad_copy(c, 0, 2 * KR), lambda: broad_copy(c, 1, 2 * KR))

    @pl.when((depth == 3) & (rows > 0))
    def _():
        for copy in edge_copies(0):
            copy.wait_send()

    @pl.when((depth == 3) & (rows < last))
    def _():
        for copy in edge_copies(1):
            copy.wait_send()

    for dest in range(1, LAYERS):
        @pl.when(depth < dest)
        def _():
            meta_copy(dest).wait_send()

    for at, l, dest in ((0, 0, 3), (0, 0, 1), (1, 1, 2), (2, 2, 3), (2, 1, 3), (1, 0, 2)):
        @pl.when(depth == at)
        def _():
            for c in range(COLORS):
                light_copy(l, c, dest).wait_send()


def body(incident, row_taps, col_taps, hogel_light, silhouette, fill_counts, hogel_index):
    left, right = dft_constants()
    anywhere = pl.BlockSpec(memory_space=pltpu.HBM)
    dma = pltpu.SemaphoreType.DMA
    return pl.pallas_call(
        kernel,
        name="hologram",
        out_shape=jax.ShapeDtypeStruct((1,) + incident.shape, BF16),
        in_specs=[anywhere] * 9,
        out_specs=pl.BlockSpec(memory_space=pltpu.VMEM),
        scratch_shapes=[
            pltpu.VMEM((2, COLORS, 2, EXT, COLS), BF16),
            pltpu.VMEM((COLORS, 2, EXT + ROWS_DEV, COLS), BF16),
            pltpu.VMEM((COLORS, 2, EXT, COLS), BF16),
            pltpu.VMEM((LAYERS, COLORS, ROWS_DEV, COLS), BF16),
            pltpu.VMEM((2, COLORS, HS, COLS), BF16),
            pltpu.VMEM((LAYERS, ROWS_DEV + HS, 128), BF16),
            pltpu.VMEM((2, HS, 128), BF16),
            pltpu.VMEM((COLORS, ROWS_DEV, COLS), F32),
            pltpu.VMEM(row_taps.shape, BF16),
            pltpu.VMEM(col_taps.shape, BF16),
            pltpu.VMEM(silhouette.shape, jnp.int32),
            pltpu.VMEM(fill_counts.shape, jnp.int32),
            pltpu.VMEM(hogel_index.shape, jnp.int32),
            pltpu.VMEM(left.shape, BF16),
            pltpu.VMEM(right.shape, BF16),
            pltpu.VMEM((16, 128), F32),
            pltpu.VMEM((NH, COLS), BF16),
            pltpu.VMEM((2, COLORS, 2 * ROWS_DEV, 128), BF16),
            pltpu.VMEM((COLORS, 2 * EXT, 2 * (EXT + ROWS_DEV)), BF16),
            pltpu.VMEM((3, COLORS, 512, 256), BF16),
            pltpu.VMEM((2, ROWS_DEV, COLS), F32),
            pltpu.VMEM((EXT, COLS), F32),
            pltpu.VMEM((COLORS, 2, ROWS_DEV, COLS), F32),
            pltpu.VMEM((COLORS, 2, EXT, COLS), F32),
            pltpu.VMEM((COLORS, 2 * ROWS_DEV, COLS + 128), BF16),
            pltpu.VMEM((COLORS, 2 * EXT, COLS + 128), BF16),
            pltpu.VMEM((2, COLORS, ROWS_DEV * TILES, 256), BF16),
            dma((13,)),
            dma((2, COLORS, 2)),
            dma((2, COLORS, 2)),
            dma((COLORS, 2)),
            dma((COLORS, 2)),
            dma((2, COLORS + 1)),
            dma((2, COLORS + 1)),
            dma((LAYERS * LAYERS, COLORS)),
            dma((LAYERS, COLORS)),
            dma((LAYERS,)),
            dma((LAYERS,)),
            pltpu.SemaphoreType.REGULAR,
        ],
        compiler_params=pltpu.CompilerParams(
            collective_id=0, has_side_effects=True, vmem_limit_bytes=40 << 20
        ),
    )(*[
        pltpu.with_memory_space_constraint(x, pltpu.HBM)
        for x in (
            incident, row_taps, col_taps, hogel_light, silhouette, fill_counts, hogel_index,
            jnp.asarray(left), jnp.asarray(right),
        )
    ])


def solution(mesh):
    placed = (
        P(None, None, "rows", None),
        P("depth", None, None, None),
        P("depth", None, None, None),
        P("depth", None, "rows", None),
        P("depth", "rows", None),
        P("depth", "rows"),
        P("depth", "rows", None),
    )
    return jax.shard_map(
        body,
        mesh=mesh,
        in_specs=placed,
        out_specs=P("depth", None, None, "rows", None),
        check_vma=False,
    )
```
